32 devices in a mesh: loop: 8 (over z, core), red: 4 (over y, x).
Axes of the slice: x: 2, y: 2, z: 4, core: 2. Of those that a mesh axis runs over, the one named last changes fastest.
Arguments:
- query_ids: int32 [512], replicated, may hold values from 0 to 8191
- layer_index: int32 [1], replicated, may hold values from 0 to 3
- gradient: bfloat16 [8192, 28672], P('loop', 'red'), may hold values from -6 to 6
- out_basis: bfloat16 [8192, 8192], P('loop'), may hold values from -0.0625 to 0.0625
- in_basis: bfloat16 [28672, 28672], P('red', 'loop'), may hold values from -0.03125 to 0.03125
- out_eigen: float32 [4, 8192], replicated, may hold values from 0.2 to 2
- in_eigen: float32 [4, 28672], P(None, 'loop'), may hold values from 0.2 to 2
Outputs:
- preconditioned: bfloat16 [512, 28672], P('loop', 'red')
The draws below stay inside these ranges and needn't reach their ends.
All inputs are finite; a program needn't handle non-finite values.
Results may differ from the reference program's by a relative error of at most 0.0055.
Values may be sent and summed in bfloat16 or wider, within the bound.
A program may use at most 192 MiB of HBM per device.

```python
import math
import jax
import jax.numpy as jnp
from jax import lax

D = 8192
FF = 28672
QUERIES = 512
LAYERS = 4


def place_ends(values, rng, low, largest):
    dims = values.shape
    index_at = [jax.random.randint(jax.random.fold_in(rng, axis), (), 0, dims[axis]) for axis in range(len(dims))]
    values = values.at[tuple(index_at)].set(low)
    longest = dims.index(max(dims))
    index_at[longest] = (index_at[longest] + 1) % dims[longest]
    return values.at[tuple(index_at)].set(largest)


def steps_of(key, dims, split, low, largest):
    level, own = 1.0, jax.random.fold_in(key, 6)
    for position, shards_of in split:
        heights = jnp.exp(jax.random.uniform(jax.random.fold_in(own, position), (shards_of,), jnp.float32, low / len(split), largest / len(split)))
        level = level * jnp.repeat(heights, dims[position] // shards_of).reshape([-1 if axis == position else 1 for axis in range(len(dims))])
    return level


def centred(key, shape, spread, most, cuts=(), dtype=jnp.bfloat16):
    values = jax.random.normal(key, shape, jnp.float32) * spread
    if len(cuts) > 0:
        values = steps_of(key, shape, cuts, -0.22, 0.18) * values
    return jnp.clip(values, min=-most, max=most).astype(dtype)


def setup_inputs(seed: int = 0) -> dict:
    splits = jax.random.split(jax.random.key(seed), 8)
    return {
        "query_ids": place_ends(jax.random.randint(splits[0], (QUERIES,), 0, D), jax.random.fold_in(splits[0], 1), 0, D - 1).astype(jnp.int32),
        "layer_index": jax.random.randint(splits[1], (1,), 0, LAYERS).astype(jnp.int32),
        "gradient": centred(splits[2], (D, FF), 1.0, 6.0, ((0, 8), (1, 4))),
        "out_basis": centred(splits[3], (D, D), D ** -0.5, 0.0625, ((0, 8),)),
        "in_basis": centred(splits[4], (FF, FF), FF ** -0.5, 0.03125, ((0, 4), (1, 8))),
        "out_eigen": jnp.clip(jnp.exp(jax.random.uniform(splits[5], (LAYERS, D), jnp.float32, math.log(0.2), math.log(2.0))), 0.2, 2.0),
        "in_eigen": jnp.clip(jnp.exp(math.log(2.0) - 2.3025851 * jax.random.uniform(splits[6], (LAYERS, FF), jnp.float32) ** steps_of(splits[6], (LAYERS, FF), ((1, 8),), -0.2, 0.2)), 0.2, 2.0),
    }


damping = 0.05


def reference(query_ids, layer_index, gradient, out_basis, in_basis, out_eigen, in_eigen):
    selected = jnp.take(out_basis, query_ids, axis=1)
    rows_w = lax.dot_general(selected, gradient, (((0,), (0,)), ((), ())), preferred_element_type=jnp.float32).astype(jnp.bfloat16)
    rotated = jnp.dot(rows_w, in_basis, preferred_element_type=jnp.float32)
    eigen_rows = jnp.take(jnp.take(out_eigen, layer_index, axis=0)[0], query_ids)
    eigen_cols = jnp.take(in_eigen, layer_index, axis=0)[0]
    scaled = (rotated / (eigen_rows[:, None] * eigen_cols[None, :] + damping)).astype(jnp.bfloat16)
    result = lax.dot_general(scaled, in_basis, (((1,), (1,)), ((), ())), preferred_element_type=jnp.float32)
    return result.astype(jnp.bfloat16)
```

```python
import jax
import jax.numpy as jnp
from jax import lax
from jax.experimental import pallas as pl
from jax.experimental.pallas import tpu as pltpu
from jax.sharding import PartitionSpec as P

damping = 0.05
QUERY_CHUNKS = 2
PIECES = 14
IN_LAG, MID_LAG, OUT_LAG, SCATTER_LAG = 1, 2, 2, 1


def piece_count(*sizes):
    count = PIECES
    while any(size % count or (size // count) % 128 for size in sizes):
        count -= 1
    return count


def make(mesh):
    loop, red = mesh.shape["loop"], mesh.shape["red"]
    chips = loop // 2
    half = chips // 2
    bits = red.bit_length() - 1
    f32, bf16 = jnp.float32, jnp.bfloat16

    def product(per, own, r, depth, rows, cols, n):
        wide, thin = rows // n, cols // n
        total = QUERY_CHUNKS * n
        sum_lag = 2 + (IN_LAG + OUT_LAG) * (half - 1) + MID_LAG
        sum_slots = sum_lag + 1
        red_lag = 2 * bits
        red_slots = red_lag + 2
        scatter_lag = 1 + (chips - 1) * SCATTER_LAG
        scatter_slots = scatter_lag + 3
        stream = per // 2
        turn_at, out_at = [], []
        for q in range(QUERY_CHUNKS):
            ready = (q + 1) * n + sum_lag
            turn_at.append(max(ready, turn_at[-1] + n) if q else ready)
            ready = turn_at[-1] + n + red_lag
            out_at.append(max(ready, out_at[-1] + n) if q else ready)
        ticks = out_at[-1] + n + scatter_lag

        def kernel(
            selected, gradient, in_basis, eigen_rows, eigen_cols, out,
            grad_tile, mine, other, swapped, arrived, crossed, sent, rows_w,
            turn_tile, part, staged, *rest,
        ):
            got, rest = rest[:bits], rest[bits:]
            (
                scaled, out_tile, omine, oother, oswapped, rsent, lsent, rgot, lgot,
                grad_sem, turn_sem, tile_sem,
                swap_s, swap_r, in_s, in_r, mid_s, mid_r, out_s, out_r, back_s, back_r,
                red_s, red_r, all_s, all_r,
                oswap_s, oswap_r, right_s, right_r, left_s, left_r,
            ) = rest
            me = lax.axis_index("loop")
            here = lax.axis_index("red")
            chip, core = me // 2, me % 2
            left = chip < half
            depth_in = jnp.where(left, chip, chips - 1 - chip)
            is_mid = depth_in == half - 1
            is_end = depth_in == 0
            partner = chip * 2 + 1 - core
            inner = jnp.where(left, me + 2, me - 2)
            outer = jnp.where(left, me - 2, me + 2)

            def remote(src, dst, s, r, k, to):
                return pltpu.make_async_remote_copy(
                    src_ref=src, dst_ref=dst, send_sem=s.at[k], recv_sem=r.at[k],
                    device_id=to, device_id_type=pl.DeviceIdType.MESH,
                )

            def span(i, size):
                return pl.ds(pl.multiple_of(i * size, size), size)

            def swap(g):
                s = g % sum_slots
                return remote(other.at[s], swapped.at[s], swap_s, swap_r, s, {"loop": partner})

            def go_in(g):
                s = g % sum_slots
                return remote(sent.at[s], arrived.at[s], in_s, in_r, s, {"loop": inner})

            def go_mid(g):
                s = g % sum_slots
                return remote(sent.at[s], crossed.at[s], mid_s, mid_r, s, {"loop": inner})

            def go_out(g):
                at = rows_w.at[g // n, pl.ds(0, own), span(g % n, wide)]
                return remote(at, at, out_s, out_r, g % sum_slots, {"loop": outer})

            def go_back(g):
                cut = span(g % n, wide)
                return remote(
                    rows_w.at[g // n, pl.ds(0, own), cut], rows_w.at[g // n, pl.ds(own, own), cut],
                    back_s, back_r, g % sum_slots, {"loop": partner},
                )

            order = [[(k + turn) % bits for k in range(bits)] for turn in range(2)]
            keep, give = [], []
            for turn in range(2):
                at = turn * stream
                keep.append([at])
                give.append([])
                for k, bit in enumerate(order[turn]):
                    size = stream >> (k + 1)
                    mine_is = (here // (1 << bit)) % 2
                    give[turn].append(at + (1 - mine_is) * size)
                    at = at + mine_is * size
                    keep[turn].append(at)

            def across(turn, k):
                bit = 1 << order[turn][k]
                up = (here // bit) % 2
                return {"red": here + bit - 2 * bit * up}

            def held(start, k):
                size = stream >> k
                return pl.ds(pl.multiple_of(start, size), size)

            def red_send(g, turn, k):
                s = g % red_slots
                return remote(
                    staged.at[s, held(give[turn][k], k + 1)], got[k].at[s, turn],
                    red_s, red_r, (k * 2 + turn) * red_slots + s, across(turn, k),
                )

            def all_send(g, turn, k):
                at = scaled.at[g // n, held(keep[turn][k + 1], k + 1), span(g % n, thin)]
                return remote(
                    at, at, all_s, all_r, (k * 2 + turn) * red_slots + g % red_slots, across(turn, k)
                )

            def out_swap(g):
                s = g % scatter_slots
                return remote(oother.at[s], oswapped.at[s], oswap_s, oswap_r, s, {"loop": partner})

            def go_right(g, b):
                s = g % scatter_slots
                return remote(
                    rsent.at[s, span(b, r)], rgot.at[s, span(b, r)], right_s, right_r,
                    s * chips + b, {"loop": me + 2},
                )

            def go_left(g, b):
                s = g % scatter_slots
                return remote(
                    lsent.at[s, span(b, r)], lgot.at[s, span(b, r)], left_s, left_r,
                    s * chips + b, {"loop": me - 2},
                )

            barrier = pltpu.get_barrier_semaphore()

            def greet(to):
                pl.semaphore_signal(
                    barrier, inc=1, device_id=to, device_id_type=pl.DeviceIdType.MESH
                )

            greet({"loop": partner})
            for k in range(bits):
                greet(across(0, k))
            pl.when(chip > 0)(lambda: greet({"loop": me - 2}))
            pl.when(chip < chips - 1)(lambda: greet({"loop": me + 2}))
            edge = (chip == 0) | (chip == chips - 1)
            pl.semaphore_wait(barrier, 1 + bits + jnp.where(edge, 1, 2))

            def fetch_grad(g):
                return pltpu.make_async_copy(
                    gradient.at[:, span(g % n, wide)], grad_tile.at[g % 2], grad_sem.at[g % 2]
                )

            def fetch_turn(g):
                return pltpu.make_async_copy(
                    in_basis.at[:, span(g % n, thin)], turn_tile.at[g % 2], turn_sem.at[g % 2]
                )

            def fetch_out(g):
                return pltpu.make_async_copy(
                    in_basis.at[span(g % n, wide)], out_tile.at[g % 2], tile_sem.at[g % 2]
                )

            def ahead(fetch, g):
                fetch(g).wait()
                pl.when(g + 1 < total)(lambda: fetch(g + 1).start())

            def rows_tile(g):
                s = g % sum_slots
                ahead(fetch_grad, g)
                whole = jnp.dot(
                    selected[g // n], grad_tile[g % 2], preferred_element_type=f32
                )
                pl.when(g >= sum_slots)(lambda: swap(g - sum_slots).wait_send())
                mine[s] = whole[:own]
                other[s] = whole[own:].astype(bf16)
                swap(g).start()

            def sum_in(g):
                s = g % sum_slots

                @pl.when(g >= sum_slots)
                def _():
                    pl.when(is_mid)(lambda: go_mid(g - sum_slots).wait_send())
                    pl.when(jnp.logical_not(is_mid))(lambda: go_in(g - sum_slots).wait_send())

                swap(g).wait_recv()

                @pl.when(is_end)
                def _():
                    value = mine[s] + swapped[s].astype(f32)
                    mine[s] = value
                    sent[s] = value.astype(bf16)

                @pl.when(jnp.logical_not(is_end))
                def _():
                    go_in(g).wait_recv()
                    value = mine[s] + swapped[s].astype(f32) + arrived[s].astype(f32)
                    mine[s] = value
                    sent[s] = value.astype(bf16)

                pl.when(is_mid)(lambda: go_mid(g).start())
                pl.when(jnp.logical_not(is_mid))(lambda: go_in(g).start())

            def sum_out(g):
                s = g % sum_slots

                @pl.when(g >= sum_slots)
                def _():
                    go_back(g - sum_slots).wait_send()
                    pl.when(jnp.logical_not(is_end))(lambda: go_out(g - sum_slots).wait_send())

                @pl.when(is_mid)
                def _():
                    go_mid(g).wait_recv()
                    value = (mine[s] + crossed[s].astype(f32)).astype(bf16)
                    rows_w[g // n, pl.ds(0, own), span(g % n, wide)] = value

                pl.when(jnp.logical_not(is_mid))(lambda: go_out(g).wait_recv())
                pl.when(jnp.logical_not(is_end))(lambda: go_out(g).start())
                go_back(g).start()

            def hand_over(g, k):
                s = g % red_slots
                for turn in range(2):
                    pl.when(g >= red_slots)(
                        lambda turn=turn: red_send(g - red_slots, turn, k).wait_send()
                    )
                    at = held(give[turn][k], k + 1)
                    staged[s, at] = part[s, at].astype(bf16)
                    red_send(g, turn, k).start()

            def turn_tile_of(g):
                s = g % red_slots
                ahead(fetch_turn, g)
                cut = rows // 4

                def some(j):
                    at = span(j, cut)
                    return jnp.dot(
                        rows_w[g // n, :, at], turn_tile[g % 2, at], preferred_element_type=f32
                    )

                part[s] = some(0)

                def more(j, c):
                    part[s] += some(j)
                    return c

                lax.fori_loop(1, 4, more, 0)
                hand_over(g, 0)

            def red_in(g, k):
                s = g % red_slots
                cut = span(g % n, thin)
                for turn in range(2):
                    red_send(g, turn, k).wait_recv()
                    at = held(keep[turn][k + 1], k + 1)
                    value = part[s, at] + got[k][s, turn].astype(f32)
                    if k + 1 < bits:
                        part[s, at] = value
                    else:
                        pl.when(g >= red_slots)(
                            lambda turn=turn: all_send(g - red_slots, turn, k).wait_send()
                        )
                        scale = eigen_rows[g // n, at] * eigen_cols[:, cut]
                        scaled[g // n, at, cut] = (value / (scale + damping)).astype(bf16)
                        all_send(g, turn, k).start()
                if k + 1 < bits:
                    hand_over(g, k + 1)

            def red_out(g, k):
                for turn in range(2):
                    all_send(g, turn, k).wait_recv()
                    if k > 0:
                        pl.when(g >= red_slots)(
                            lambda turn=turn: all_send(g - red_slots, turn, k - 1).wait_send()
                        )
                        all_send(g, turn, k - 1).start()

            def out_tile_of(g):
                s = g % scatter_slots
                ahead(fetch_out, g)
                pl.when(g >= scatter_slots)(lambda: out_swap(g - scatter_slots).wait_send())
                whole = lax.dot_general(
                    scaled[g // n], out_tile[g % 2], (((1,), (1,)), ((), ())),
                    preferred_element_type=f32,
                )
                omine[s] = whole[:own]
                oother[s] = whole[own:].astype(bf16)
                out_swap(g).start()

            def each(start, stop, f):
                lax.fori_loop(start, stop, lambda b, c: (f(b), c)[1], 0)

            def chip_sum(g):
                s = g % scatter_slots
                out_swap(g).wait_recv()
                omine[s] += oswapped[s].astype(f32)

            def flow(g, go, send, get, first, start, stop):
                s = g % scatter_slots

                @pl.when(first)
                def _():
                    def plain(b):
                        pl.when(g >= scatter_slots)(lambda: go(g - scatter_slots, b).wait_send())
                        send[s, span(b, r)] = omine[s, span(b, r)].astype(bf16)
                        go(g, b).start()

                    each(start, stop, plain)

                @pl.when(jnp.logical_not(first))
                def _():
                    go(g, chip).wait_recv()
                    mid = span(chip, r)

                    def through(b):
                        pl.when(g >= scatter_slots)(lambda: go(g - scatter_slots, b).wait_send())
                        go(g, b).wait_recv()
                        at = span(b, r)
                        send[s, at] = (omine[s, at] + get[s, at].astype(f32)).astype(bf16)
                        go(g, b).start()

                    each(start, stop, through)
                    omine[s, mid] += get[s, mid].astype(f32)

            def finish(g):
                s = g % scatter_slots
                out[span(g // n, r), span(g % n, wide)] = omine[s, span(chip, r)].astype(bf16)

            def when(t, starts, lag, f):
                u = t - lag
                late = u >= starts[1]
                i = u - jnp.where(late, starts[1], starts[0])
                g = i + jnp.where(late, n, 0)
                pl.when((i >= 0) & (i < n))(lambda: f(g))

            fetch_grad(0).start()
            fetch_turn(0).start()
            fetch_out(0).start()
            row_at = [0, n]

            def tick(t):
                when(t, row_at, 0, rows_tile)
                when(t, turn_at, 0, turn_tile_of)
                when(t, out_at, 0, out_tile_of)
                when(t, row_at, 1 + IN_LAG * depth_in, sum_in)
                mid_at = 1 + IN_LAG * (half - 1) + MID_LAG
                when(t, row_at, mid_at + OUT_LAG * (half - 1 - depth_in), sum_out)
                when(t, row_at, sum_lag, lambda g: go_back(g).wait_recv())
                when(t, out_at, 1, chip_sum)
                when(
                    t, out_at, 1 + SCATTER_LAG * chip,
                    lambda g: flow(g, go_right, rsent, rgot, chip == 0, chip + 1, chips),
                )
                when(
                    t, out_at, 1 + SCATTER_LAG * (chips - 1 - chip),
                    lambda g: flow(g, go_left, lsent, lgot, chip == chips - 1, 0, chip),
                )
                for k in range(bits):
                    when(t, turn_at, 1 + k, lambda g, k=k: red_in(g, k))
                for k in range(bits):
                    when(t, turn_at, 1 + bits + k, lambda g, k=k: red_out(g, bits - 1 - k))
                last = 1 + SCATTER_LAG * jnp.maximum(chip, chips - 1 - chip)
                when(t, out_at, last, finish)

            each(0, ticks, tick)

            def drain_sum(g):
                swap(g).wait_send()
                go_back(g).wait_send()
                pl.when(is_mid)(lambda: go_mid(g).wait_send())
                pl.when(jnp.logical_not(is_mid))(lambda: go_in(g).wait_send())
                pl.when(jnp.logical_not(is_end))(lambda: go_out(g).wait_send())

            def drain_red(g):
                for turn in range(2):
                    for k in range(bits):
                        red_send(g, turn, k).wait_send()
                        all_send(g, turn, k).wait_send()

            def drain_scatter(g):
                out_swap(g).wait_send()
                each(chip + 1, chips, lambda b: go_right(g, b).wait_send())
                each(0, chip, lambda b: go_left(g, b).wait_send())

            each(max(0, total - sum_slots), total, drain_sum)
            each(max(0, total - red_slots), total, drain_red)
            each(max(0, total - scatter_slots), total, drain_scatter)

        vmem = pl.BlockSpec(memory_space=pltpu.VMEM)
        hbm = pl.BlockSpec(memory_space=pl.ANY)

        def sems(count):
            return pltpu.SemaphoreType.DMA((count,))

        def slots(count, *shape):
            return pltpu.VMEM((count, *shape), bf16)

        return pl.pallas_call(
            kernel,
            out_shape=jax.ShapeDtypeStruct((QUERY_CHUNKS * r, rows), bf16),
            in_specs=[vmem, hbm, hbm, vmem, vmem],
            out_specs=vmem,
            scratch_shapes=[slots(2, depth, wide), pltpu.VMEM((sum_slots, own, wide), f32)]
            + [slots(sum_slots, own, wide)] * 5
            + [
                slots(QUERY_CHUNKS, per, rows),
                slots(2, rows, thin),
                pltpu.VMEM((red_slots, per, thin), f32),
                slots(red_slots, per, thin),
            ]
            + [slots(red_slots, 2, stream >> (k + 1), thin) for k in range(bits)]
            + [
                slots(QUERY_CHUNKS, per, cols),
                slots(2, wide, cols),
                pltpu.VMEM((scatter_slots, own, wide), f32),
            ]
            + [slots(scatter_slots, own, wide)] * 6
            + [sems(2)] * 3
            + [sems(sum_slots)] * 10
            + [sems(2 * bits * red_slots)] * 4
            + [sems(scatter_slots)] * 2
            + [sems(scatter_slots * chips)] * 4,
            compiler_params=pltpu.CompilerParams(
                collective_id=0, has_side_effects=True, vmem_limit_bytes=62 * 1024 * 1024
            ),
        )

    def per_device(query_ids, layer_index, gradient, out_basis, in_basis, out_eigen, in_eigen):
        core = lax.axis_index("loop") % 2
        queries = query_ids.shape[0]
        depth, rows = gradient.shape
        cols = in_basis.shape[1]
        r = queries // loop // QUERY_CHUNKS
        per = queries // QUERY_CHUNKS
        ids = query_ids.reshape(chips, 2, QUERY_CHUNKS, r).transpose(2, 1, 0, 3)
        ids = jnp.where(core == 0, ids, ids[:, ::-1]).reshape(-1)
        out_row = lax.dynamic_index_in_dim(out_eigen, layer_index[0], 0, keepdims=False)
        eigen_cols = lax.dynamic_index_in_dim(in_eigen, layer_index[0], 0)
        eigen_rows = jnp.take(out_row, ids).reshape(QUERY_CHUNKS, per, 1)
        every = lax.broadcasted_iota(jnp.int32, (queries, out_basis.shape[1]), 1)
        selected = lax.dot_general(
            (ids[:, None] == every).astype(bf16), out_basis,
            (((1,), (1,)), ((), ())), preferred_element_type=f32,
        ).astype(bf16)
        selected = selected.reshape(QUERY_CHUNKS, per, depth)
        run = product(per, per // 2, r, depth, rows, cols, piece_count(rows, cols))
        return run(selected, gradient, in_basis, eigen_rows, eigen_cols)

    return per_device


def solution(mesh):
    return jax.shard_map(
        make(mesh),
        mesh=mesh,
        in_specs=(
            P(),
            P(),
            P("loop", "red"),
            P("loop", None),
            P("red", "loop"),
            P(),
            P(None, "loop"),
        ),
        out_specs=P("loop", "red"),
        check_vma=False,
    )
```

```python
import jax
import jax.numpy as jnp
from jax import lax
from jax.experimental import pallas as pl
from jax.experimental.pallas import tpu as pltpu
from jax.sharding import PartitionSpec as P

damping = 0.05
QUERY_CHUNKS = 2
PIECES = 14
IN_LAG, MID_LAG, OUT_LAG, SCATTER_LAG = 2, 2, 2, 2
BUFFERS = 3
DEPTHS = 2
TURN_RATE = (1, 1)
RED_LAG = 2


def piece_count(*sizes):
    count = PIECES
    while any(size % count or (size // count) % 128 for size in sizes):
        count -= 1
    return count


def make(mesh):
    loop, red = mesh.shape["loop"], mesh.shape["red"]
    chips = loop // 2
    half = chips // 2
    bits = red.bit_length() - 1
    f32, bf16 = jnp.float32, jnp.bfloat16

    def product(per, own, r, depth, rows, cols, n):
        wide, thin = rows // n, cols // n
        total = QUERY_CHUNKS * n
        sum_lag = 2 + (IN_LAG + OUT_LAG) * (half - 1) + MID_LAG
        sum_slots = sum_lag + 1
        red_lag = 2 * bits * RED_LAG
        red_slots = -(-(red_lag + 2) * TURN_RATE[0] // TURN_RATE[1])
        scatter_lag = 1 + (chips - 1) * SCATTER_LAG
        scatter_slots = scatter_lag + 3
        stream = per // 2
        turn_at, out_at = [], []
        for q in range(QUERY_CHUNKS):
            ready = (q + 1) * n + sum_lag
            turn_at.append(ready)
            num, den = (1, 1) if q else TURN_RATE
            ready = turn_at[-1] + -(-n * den // num) + red_lag
            out_at.append(max(ready, out_at[-1] + n) if q else ready)
        ticks = out_at[-1] + n + scatter_lag

        def kernel(
            selected, gradient, in_basis, eigen_rows, eigen_cols, out,
            grad_tile, mine, other, swapped, arrived, crossed, sent, rows_w,
            turn_tile, part, staged, *rest,
        ):
            got, rest = rest[:bits], rest[bits:]
            (
                scaled, out_tile, omine, oother, oswapped, rsent, lsent, rgot, lgot,
                grad_sem, turn_sem, tile_sem,
                swap_s, swap_r, in_s, in_r, mid_s, mid_r, out_s, out_r, back_s, back_r,
                red_s, red_r, all_s, all_r,
                oswap_s, oswap_r, right_s, right_r, left_s, left_r,
            ) = rest
            me = lax.axis_index("loop")
            here = lax.axis_index("red")
            chip, core = me // 2, me % 2
            left = chip < half
            depth_in = jnp.where(left, chip, chips - 1 - chip)
            is_mid = depth_in == half - 1
            is_end = depth_in == 0
            partner = chip * 2 + 1 - core
            inner = jnp.where(left, me + 2, me - 2)
            outer = jnp.where(left, me - 2, me + 2)

            def remote(src, dst, s, r, k, to):
                return pltpu.make_async_remote_copy(
                    src_ref=src, dst_ref=dst, send_sem=s.at[k], recv_sem=r.at[k],
                    device_id=to, device_id_type=pl.DeviceIdType.MESH,
                )

            def span(i, size):
                return pl.ds(pl.multiple_of(i * size, size), size)

            def swap(g):
                s = g % sum_slots
                return remote(other.at[s], swapped.at[s], swap_s, swap_r, s, {"loop": partner})

            def go_in(g):
                s = g % sum_slots
                return remote(sent.at[s], arrived.at[s], in_s, in_r, s, {"loop": inner})

            def go_mid(g):
                s = g % sum_slots
                return remote(sent.at[s], crossed.at[s], mid_s, mid_r, s, {"loop": inner})

            def go_out(g):
                at = rows_w.at[g // n, pl.ds(0, own), span(g % n, wide)]
                return remote(at, at, out_s, out_r, g % sum_slots, {"loop": outer})

            def go_back(g):
                cut = span(g % n, wide)
                return remote(
                    rows_w.at[g // n, pl.ds(0, own), cut], rows_w.at[g // n, pl.ds(own, own), cut],
                    back_s, back_r, g % sum_slots, {"loop": partner},
                )

            order = [[(k + turn) % bits for k in range(bits)] for turn in range(2)]
            keep, give = [], []
            for turn in range(2):
                at = turn * stream
                keep.append([at])
                give.append([])
                for k, bit in enumerate(order[turn]):
                    size = stream >> (k + 1)
                    mine_is = (here // (1 << bit)) % 2
                    give[turn].append(at + (1 - mine_is) * size)
                    at = at + mine_is * size
                    keep[turn].append(at)

            def across(turn, k):
                bit = 1 << order[turn][k]
                up = (here // bit) % 2
                return {"red": here + bit - 2 * bit * up}

            def held(start, k):
                size = stream >> k
                return pl.ds(pl.multiple_of(start, size), size)

            def red_send(g, turn, k):
                s = g % red_slots
                return remote(
                    staged.at[s, held(give[turn][k], k + 1)], got[k].at[s, turn],
                    red_s, red_r, (k * 2 + turn) * red_slots + s, across(turn, k),
                )

            def all_send(g, turn, k):
                at = scaled.at[g // n, held(keep[turn][k + 1], k + 1), span(g % n, thin)]
                return remote(
                    at, at, all_s, all_r, (k * 2 + turn) * red_slots + g % red_slots, across(turn, k)
                )

            def out_swap(g):
                s = g % scatter_slots
                return remote(oother.at[s], oswapped.at[s], oswap_s, oswap_r, s, {"loop": partner})

            def go_right(g, b):
                s = g % scatter_slots
                return remote(
                    rsent.at[s, span(b, r)], rgot.at[s, span(b, r)], right_s, right_r,
                    s * chips + b, {"loop": me + 2},
                )

            def go_left(g, b):
                s = g % scatter_slots
                return remote(
                    lsent.at[s, span(b, r)], lgot.at[s, span(b, r)], left_s, left_r,
                    s * chips + b, {"loop": me - 2},
                )

            barrier = pltpu.get_barrier_semaphore()

            def greet(to):
                pl.semaphore_signal(
                    barrier, inc=1, device_id=to, device_id_type=pl.DeviceIdType.MESH
                )

            greet({"loop": partner})
            for k in range(bits):
                greet(across(0, k))
            pl.when(chip > 0)(lambda: greet({"loop": me - 2}))
            pl.when(chip < chips - 1)(lambda: greet({"loop": me + 2}))
            edge = (chip == 0) | (chip == chips - 1)
            pl.semaphore_wait(barrier, 1 + bits + jnp.where(edge, 1, 2))

            def fetch_grad(g):
                return pltpu.make_async_copy(
                    gradient.at[:, span(g % n, wide)], grad_tile.at[g % BUFFERS], grad_sem.at[g % BUFFERS]
                )

            def fetch_turn(g):
                return pltpu.make_async_copy(
                    in_basis.at[:, span(g % n, thin)], turn_tile.at[g % BUFFERS], turn_sem.at[g % BUFFERS]
                )

            def fetch_out(g):
                return pltpu.make_async_copy(
                    in_basis.at[span(g % n, wide)], out_tile.at[g % BUFFERS], tile_sem.at[g % BUFFERS]
                )

            def ahead(fetch, g):
                fetch(g).wait()
                more = g + BUFFERS - 1
                pl.when(more < total)(lambda: fetch(more).start())

            def rows_tile(g):
                s = g % sum_slots
                ahead(fetch_grad, g)
                whole = jnp.dot(
                    selected[g // n], grad_tile[g % BUFFERS], preferred_element_type=f32
                )
                pl.when(g >= sum_slots)(lambda: swap(g - sum_slots).wait_send())
                mine[s] = whole[:own]
                other[s] = whole[own:].astype(bf16)
                swap(g).start()

            def sum_in(g):
                s = g % sum_slots

                @pl.when(g >= sum_slots)
                def _():
                    pl.when(is_mid)(lambda: go_mid(g - sum_slots).wait_send())
                    pl.when(jnp.logical_not(is_mid))(lambda: go_in(g - sum_slots).wait_send())

                swap(g).wait_recv()

                @pl.when(is_end)
                def _():
                    value = mine[s] + swapped[s].astype(f32)
                    mine[s] = value
                    sent[s] = value.astype(bf16)

                @pl.when(jnp.logical_not(is_end))
                def _():
                    go_in(g).wait_recv()
                    value = mine[s] + swapped[s].astype(f32) + arrived[s].astype(f32)
                    mine[s] = value
                    sent[s] = value.astype(bf16)

                pl.when(is_mid)(lambda: go_mid(g).start())
                pl.when(jnp.logical_not(is_mid))(lambda: go_in(g).start())

            def sum_out(g):
                s = g % sum_slots

                @pl.when(g >= sum_slots)
                def _():
                    go_back(g - sum_slots).wait_send()
                    pl.when(jnp.logical_not(is_end))(lambda: go_out(g - sum_slots).wait_send())

                @pl.when(is_mid)
                def _():
                    go_mid(g).wait_recv()
                    value = (mine[s] + crossed[s].astype(f32)).astype(bf16)
                    rows_w[g // n, pl.ds(0, own), span(g % n, wide)] = value

                pl.when(jnp.logical_not(is_mid))(lambda: go_out(g).wait_recv())
                pl.when(jnp.logical_not(is_end))(lambda: go_out(g).start())
                go_back(g).start()

            def hand_over(g, k):
                s = g % red_slots
                for turn in range(2):
                    pl.when(g >= red_slots)(
                        lambda turn=turn: red_send(g - red_slots, turn, k).wait_send()
                    )
                    at = held(give[turn][k], k + 1)
                    staged[s, at] = part[s, at].astype(bf16)
                    red_send(g, turn, k).start()

            def turn_tile_of(g):
                s = g % red_slots
                ahead(fetch_turn, g)
                cut = rows // DEPTHS

                def some(j):
                    at = span(j, cut)
                    return jnp.dot(
                        rows_w[g // n, :, at], turn_tile[g % BUFFERS, at], preferred_element_type=f32
                    )

                part[s] = some(0)

                def more(j, c):
                    part[s] += some(j)
                    return c

                lax.fori_loop(1, DEPTHS, more, 0)
                hand_over(g, 0)

            def red_in(g, k):
                s = g % red_slots
                cut = span(g % n, thin)
                for turn in range(2):
                    red_send(g, turn, k).wait_recv()
                    at = held(keep[turn][k + 1], k + 1)
                    value = part[s, at] + got[k][s, turn].astype(f32)
                    if k + 1 < bits:
                        part[s, at] = value
                    else:
                        pl.when(g >= red_slots)(
                            lambda turn=turn: all_send(g - red_slots, turn, k).wait_send()
                        )
                        scale = eigen_rows[g // n, at] * eigen_cols[:, cut]
                        scaled[g // n, at, cut] = (value / (scale + damping)).astype(bf16)
                        all_send(g, turn, k).start()
                if k + 1 < bits:
                    hand_over(g, k + 1)

            def red_out(g, k):
                for turn in range(2):
                    all_send(g, turn, k).wait_recv()
                    if k > 0:
                        pl.when(g >= red_slots)(
                            lambda turn=turn: all_send(g - red_slots, turn, k - 1).wait_send()
                        )
                        all_send(g, turn, k - 1).start()

            def out_tile_of(g):
                s = g % scatter_slots
                ahead(fetch_out, g)
                pl.when(g >= scatter_slots)(lambda: out_swap(g - scatter_slots).wait_send())
                whole = lax.dot_general(
                    scaled[g // n], out_tile[g % BUFFERS], (((1,), (1,)), ((), ())),
                    preferred_element_type=f32,
                )
                omine[s] = whole[:own]
                oother[s] = whole[own:].astype(bf16)
                out_swap(g).start()

            def each(start, stop, f):
                lax.fori_loop(start, stop, lambda b, c: (f(b), c)[1], 0)

            def chip_sum(g):
                s = g % scatter_slots
                out_swap(g).wait_recv()
                omine[s] += oswapped[s].astype(f32)

            def flow(g, go, send, get, first, start, stop):
                s = g % scatter_slots

                @pl.when(first)
                def _():
                    def plain(b):
                        pl.when(g >= scatter_slots)(lambda: go(g - scatter_slots, b).wait_send())
                        send[s, span(b, r)] = omine[s, span(b, r)].astype(bf16)
                        go(g, b).start()

                    each(start, stop, plain)

                @pl.when(jnp.logical_not(first))
                def _():
                    go(g, chip).wait_recv()
                    mid = span(chip, r)

                    def through(b):
                        pl.when(g >= scatter_slots)(lambda: go(g - scatter_slots, b).wait_send())
                        go(g, b).wait_recv()
                        at = span(b, r)
                        send[s, at] = (omine[s, at] + get[s, at].astype(f32)).astype(bf16)
                        go(g, b).start()

                    each(start, stop, through)
                    omine[s, mid] += get[s, mid].astype(f32)

            def finish(g):
                s = g % scatter_slots
                out[span(g // n, r), span(g % n, wide)] = omine[s, span(chip, r)].astype(bf16)

            def when(t, starts, lag, f):
                u = t - lag
                for q in range(QUERY_CHUNKS):
                    num, den = TURN_RATE if starts is turn_at and q == 0 else (1, 1)

                    def first(u):
                        return jnp.clip(u - starts[q], 0, n) * num // den

                    lo, hi = jnp.minimum(first(u), n), jnp.minimum(first(u + 1), n)
                    each(lo + q * n, hi + q * n, f)

            for g in range(BUFFERS - 1):
                for fetch in (fetch_grad, fetch_turn, fetch_out):
                    fetch(g).start()

            row_at = [q * n for q in range(QUERY_CHUNKS)]

            def tick(t):
                when(t, row_at, 0, rows_tile)
                when(t, turn_at, 0, turn_tile_of)
                when(t, out_at, 0, out_tile_of)
                when(t, row_at, 1 + IN_LAG * depth_in, sum_in)
                mid_at = 1 + IN_LAG * (half - 1) + MID_LAG
                when(t, row_at, mid_at + OUT_LAG * (half - 1 - depth_in), sum_out)
                when(t, row_at, sum_lag, lambda g: go_back(g).wait_recv())
                when(t, out_at, 1, chip_sum)
                when(
                    t, out_at, 1 + SCATTER_LAG * chip,
                    lambda g: flow(g, go_right, rsent, rgot, chip == 0, chip + 1, chips),
                )
                when(
                    t, out_at, 1 + SCATTER_LAG * (chips - 1 - chip),
                    lambda g: flow(g, go_left, lsent, lgot, chip == chips - 1, 0, chip),
                )
                for k in range(bits):
                    when(t, turn_at, RED_LAG * (1 + k), lambda g, k=k: red_in(g, k))
                for k in range(bits):
                    when(
                        t, turn_at, RED_LAG * (1 + bits + k),
                        lambda g, k=k: red_out(g, bits - 1 - k),
                    )
                last = 1 + SCATTER_LAG * jnp.maximum(chip, chips - 1 - chip)
                when(t, out_at, last, finish)

            each(0, ticks, tick)

            def drain_sum(g):
                swap(g).wait_send()
                go_back(g).wait_send()
                pl.when(is_mid)(lambda: go_mid(g).wait_send())
                pl.when(jnp.logical_not(is_mid))(lambda: go_in(g).wait_send())
                pl.when(jnp.logical_not(is_end))(lambda: go_out(g).wait_send())

            def drain_red(g):
                for turn in range(2):
                    for k in range(bits):
                        red_send(g, turn, k).wait_send()
                        all_send(g, turn, k).wait_send()

            def drain_scatter(g):
                out_swap(g).wait_send()
                each(chip + 1, chips, lambda b: go_right(g, b).wait_send())
                each(0, chip, lambda b: go_left(g, b).wait_send())

            each(max(0, total - sum_slots), total, drain_sum)
            each(max(0, total - red_slots), total, drain_red)
            each(max(0, total - scatter_slots), total, drain_scatter)

        vmem = pl.BlockSpec(memory_space=pltpu.VMEM)
        hbm = pl.BlockSpec(memory_space=pl.ANY)

        def sems(count):
            return pltpu.SemaphoreType.DMA((count,))

        def slots(count, *shape):
            return pltpu.VMEM((count, *shape), bf16)

        return pl.pallas_call(
            kernel,
            out_shape=jax.ShapeDtypeStruct((QUERY_CHUNKS * r, rows), bf16),
            in_specs=[vmem, hbm, hbm, vmem, vmem],
            out_specs=vmem,
            scratch_shapes=[slots(BUFFERS, depth, wide), pltpu.VMEM((sum_slots, own, wide), f32)]
            + [slots(sum_slots, own, wide)] * 5
            + [
                slots(QUERY_CHUNKS, per, rows),
                slots(BUFFERS, rows, thin),
                pltpu.VMEM((red_slots, per, thin), f32),
                slots(red_slots, per, thin),
            ]
            + [slots(red_slots, 2, stream >> (k + 1), thin) for k in range(bits)]
            + [
                slots(QUERY_CHUNKS, per, cols),
                slots(BUFFERS, wide, cols),
                pltpu.VMEM((scatter_slots, own, wide), f32),
            ]
            + [slots(scatter_slots, own, wide)] * 6
            + [sems(BUFFERS)] * 3
            + [sems(sum_slots)] * 10
            + [sems(2 * bits * red_slots)] * 4
            + [sems(scatter_slots)] * 2
            + [sems(scatter_slots * chips)] * 4,
            compiler_params=pltpu.CompilerParams(
                collective_id=0, has_side_effects=True, vmem_limit_bytes=62 * 1024 * 1024
            ),
        )

    def per_device(query_ids, layer_index, gradient, out_basis, in_basis, out_eigen, in_eigen):
        core = lax.axis_index("loop") % 2
        queries = query_ids.shape[0]
        depth, rows = gradient.shape
        cols = in_basis.shape[1]
        r = queries // loop // QUERY_CHUNKS
        per = queries // QUERY_CHUNKS
        ids = query_ids.reshape(chips, 2, QUERY_CHUNKS, r).transpose(2, 1, 0, 3)
        ids = jnp.where(core == 0, ids, ids[:, ::-1]).reshape(-1)
        out_row = lax.dynamic_index_in_dim(out_eigen, layer_index[0], 0, keepdims=False)
        eigen_cols = lax.dynamic_index_in_dim(in_eigen, layer_index[0], 0)
        eigen_rows = jnp.take(out_row, ids).reshape(QUERY_CHUNKS, per, 1)
        every = lax.broadcasted_iota(jnp.int32, (queries, out_basis.shape[1]), 1)
        selected = lax.dot_general(
            (ids[:, None] == every).astype(bf16), out_basis,
            (((1,), (1,)), ((), ())), preferred_element_type=f32,
        ).astype(bf16)
        selected = selected.reshape(QUERY_CHUNKS, per, depth)
        run = product(per, per // 2, r, depth, rows, cols, piece_count(rows, cols))
        return run(selected, gradient, in_basis, eigen_rows, eigen_cols)

    return per_device


def solution(mesh):
    return jax.shard_map(
        make(mesh),
        mesh=mesh,
        in_specs=(
            P(),
            P(),
            P("loop", "red"),
            P("loop", None),
            P("red", "loop"),
            P(),
            P(None, "loop"),
        ),
        out_specs=P("loop", "red"),
        check_vma=False,
    )
```

```python
import jax
import jax.numpy as jnp
from jax import lax
from jax.experimental import pallas as pl
from jax.experimental.pallas import tpu as pltpu
from jax.sharding import PartitionSpec as P

damping = 0.05
QUERY_CHUNKS = 2
PIECES = 14
IN_LAG, MID_LAG, OUT_LAG, SCATTER_LAG = 2, 2, 2, 2
BUFFERS = 3
PICK_BUFFERS, TURN_BUFFERS, OUT_BUFFERS = 6, 3, 2
DEPTHS = 2
TURN_RATE = (1, 1)
RED_LAG = 2


def piece_count(*sizes):
    count = PIECES
    while any(size % count or (size // count) % 128 for size in sizes):
        count -= 1
    return count


def make(mesh):
    loop, red = mesh.shape["loop"], mesh.shape["red"]
    chips = loop // 2
    half = chips // 2
    bits = red.bit_length() - 1
    f32, bf16 = jnp.float32, jnp.bfloat16

    def product(per, own, r, depth, units, rows, cols, n):
        wide, thin = rows // n, cols // n
        total = QUERY_CHUNKS * n
        picks = units // wide
        sum_lag = 2 + (IN_LAG + OUT_LAG) * (half - 1) + MID_LAG
        sum_slots = sum_lag + 1
        red_lag = 2 * bits * RED_LAG
        red_slots = -(-(red_lag + 1) * TURN_RATE[0] // TURN_RATE[1])
        scatter_lag = 1 + (chips - 1) * SCATTER_LAG
        scatter_slots = scatter_lag + 1
        stream = per // 2
        turn_at, out_at = [], []
        for q in range(QUERY_CHUNKS):
            ready = (q + 1) * n + sum_lag
            turn_at.append(ready)
            num, den = (1, 1) if q else TURN_RATE
            ready = turn_at[-1] + -(-n * den // num) + red_lag
            out_at.append(max(ready, out_at[-1] + n) if q else ready)
        ticks = out_at[-1] + n + scatter_lag

        def kernel(
            layer, ids, gradient, out_basis, in_basis, out_eigen, in_eigen, out,
            selected, out_row, in_row, eigen_sum, eigen_rows, pick_tile, grad_tile, mine, other, swapped, arrived, crossed, sent, rows_w,
            turn_tile, part, staged, *rest,
        ):
            got, rest = rest[:bits], rest[bits:]
            (
                scaled, out_tile, omine, oother, oswapped, rsent, lsent, rgot, lgot,
                pick_sem, grad_sem, turn_sem, tile_sem,
                swap_s, swap_r, in_s, in_r, mid_s, mid_r, out_s, out_r, back_s, back_r,
                red_s, red_r, all_s, all_r,
                oswap_s, oswap_r, right_s, right_r, left_s, left_r,
            ) = rest
            me = lax.axis_index("loop")
            here = lax.axis_index("red")
            chip, core = me // 2, me % 2
            left = chip < half
            depth_in = jnp.where(left, chip, chips - 1 - chip)
            is_mid = depth_in == half - 1
            is_end = depth_in == 0
            partner = chip * 2 + 1 - core
            inner = jnp.where(left, me + 2, me - 2)
            outer = jnp.where(left, me - 2, me + 2)

            def remote(src, dst, s, r, k, to):
                return pltpu.make_async_remote_copy(
                    src_ref=src, dst_ref=dst, send_sem=s.at[k], recv_sem=r.at[k],
                    device_id=to, device_id_type=pl.DeviceIdType.MESH,
                )

            def span(i, size):
                return pl.ds(pl.multiple_of(i * size, size), size)

            def swap(g):
                s = g % sum_slots
                return remote(other.at[s], swapped.at[s], swap_s, swap_r, s, {"loop": partner})

            def go_in(g):
                s = g % sum_slots
                return remote(sent.at[s], arrived.at[s], in_s, in_r, s, {"loop": inner})

            def go_mid(g):
                s = g % sum_slots
                return remote(sent.at[s], crossed.at[s], mid_s, mid_r, s, {"loop": inner})

            def go_out(g):
                at = rows_w.at[g // n, pl.ds(0, own), span(g % n, wide)]
                return remote(at, at, out_s, out_r, g % sum_slots, {"loop": outer})

            def go_back(g):
                cut = span(g % n, wide)
                return remote(
                    rows_w.at[g // n, pl.ds(0, own), cut], rows_w.at[g // n, pl.ds(own, own), cut],
                    back_s, back_r, g % sum_slots, {"loop": partner},
                )

            order = [[(k + turn) % bits for k in range(bits)] for turn in range(2)]
            keep, give = [], []
            for turn in range(2):
                at = turn * stream
                keep.append([at])
                give.append([])
                for k, bit in enumerate(order[turn]):
                    size = stream >> (k + 1)
                    mine_is = (here // (1 << bit)) % 2
                    give[turn].append(at + (1 - mine_is) * size)
                    at = at + mine_is * size
                    keep[turn].append(at)

            def across(turn, k):
                bit = 1 << order[turn][k]
                up = (here // bit) % 2
                return {"red": here + bit - 2 * bit * up}

            def held(start, k):
                size = stream >> k
                return pl.ds(pl.multiple_of(start, size), size)

            def red_send(g, turn, k):
                s = g % red_slots
                return remote(
                    staged.at[s, held(give[turn][k], k + 1)], got[k].at[s, turn],
                    red_s, red_r, (k * 2 + turn) * red_slots + s, across(turn, k),
                )

            def all_send(g, turn, k):
                at = scaled.at[g // n, held(keep[turn][k + 1], k + 1), span(g % n, thin)]
                return remote(
                    at, at, all_s, all_r, (k * 2 + turn) * red_slots + g % red_slots, across(turn, k)
                )

            def out_swap(g):
                s = g % scatter_slots
                return remote(oother.at[s], oswapped.at[s], oswap_s, oswap_r, s, {"loop": partner})

            def go_right(g, b):
                s = g % scatter_slots
                return remote(
                    rsent.at[s, span(b, r)], rgot.at[s, span(b, r)], right_s, right_r,
                    s * chips + b, {"loop": me + 2},
                )

            def go_left(g, b):
                s = g % scatter_slots
                return remote(
                    lsent.at[s, span(b, r)], lgot.at[s, span(b, r)], left_s, left_r,
                    s * chips + b, {"loop": me - 2},
                )

            barrier = pltpu.get_barrier_semaphore()

            def greet(to):
                pl.semaphore_signal(
                    barrier, inc=1, device_id=to, device_id_type=pl.DeviceIdType.MESH
                )

            greet({"loop": partner})
            for k in range(bits):
                greet(across(0, k))
            pl.when(chip > 0)(lambda: greet({"loop": me - 2}))
            pl.when(chip < chips - 1)(lambda: greet({"loop": me + 2}))
            def fetch_grad(g):
                return pltpu.make_async_copy(
                    gradient.at[:, span(g % n, wide)], grad_tile.at[g % BUFFERS], grad_sem.at[g % BUFFERS]
                )

            def fetch_turn(g):
                return pltpu.make_async_copy(
                    in_basis.at[:, span(g % n, thin)], turn_tile.at[g % TURN_BUFFERS], turn_sem.at[g % TURN_BUFFERS]
                )

            def fetch_out(g):
                return pltpu.make_async_copy(
                    in_basis.at[span(g % n, wide)], out_tile.at[g % OUT_BUFFERS], tile_sem.at[g % OUT_BUFFERS]
                )

            def fetch_pick(g):
                return pltpu.make_async_copy(
                    out_basis.at[:, span(g % picks, wide)],
                    pick_tile.at[g % PICK_BUFFERS], pick_sem.at[g % PICK_BUFFERS],
                )

            def ahead(fetch, g, buffers, total=total):
                fetch(g).wait()
                more = g + buffers - 1
                pl.when(more < total)(lambda: fetch(more).start())

            def pick(g):
                q, k = g // picks, g % picks
                ahead(fetch_pick, g, PICK_BUFFERS, QUERY_CHUNKS * picks)
                at = lax.broadcasted_iota(jnp.int32, (per, wide), 1) + k * wide
                hot = ids[q] == at
                values = lax.dot_general(
                    hot.astype(bf16), pick_tile[g % PICK_BUFFERS], (((1,), (1,)), ((), ())),
                    preferred_element_type=f32,
                ).astype(bf16)
                eigen = jnp.where(hot, out_row[:, span(k, wide)], 0.0)
                eigen = sum(eigen[:, c : c + 128] for c in range(0, wide, 128))

                @pl.when(k == 0)
                def _():
                    selected[q] = values
                    eigen_sum[...] = eigen

                @pl.when(k > 0)
                def _():
                    selected[q] += values
                    eigen_sum[...] += eigen

                @pl.when(k == picks - 1)
                def _():
                    eigen_rows[q] = jnp.sum(eigen_sum[...], axis=1, keepdims=True)

            def rows_tile(g):
                s = g % sum_slots
                ahead(fetch_grad, g, BUFFERS)
                whole = jnp.dot(
                    selected[g // n], grad_tile[g % BUFFERS], preferred_element_type=f32
                )
                pl.when(g >= sum_slots)(lambda: swap(g - sum_slots).wait_send())
                mine[s] = whole[:own]
                other[s] = whole[own:].astype(bf16)
                swap(g).start()

            def sum_in(g):
                s = g % sum_slots

                @pl.when(g >= sum_slots)
                def _():
                    pl.when(is_mid)(lambda: go_mid(g - sum_slots).wait_send())
                    pl.when(jnp.logical_not(is_mid))(lambda: go_in(g - sum_slots).wait_send())

                swap(g).wait_recv()

                @pl.when(is_end)
                def _():
                    value = mine[s] + swapped[s].astype(f32)
                    mine[s] = value
                    sent[s] = value.astype(bf16)

                @pl.when(jnp.logical_not(is_end))
                def _():
                    go_in(g).wait_recv()
                    value = mine[s] + swapped[s].astype(f32) + arrived[s].astype(f32)
                    mine[s] = value
                    sent[s] = value.astype(bf16)

                pl.when(is_mid)(lambda: go_mid(g).start())
                pl.when(jnp.logical_not(is_mid))(lambda: go_in(g).start())

            def sum_out(g):
                s = g % sum_slots

                @pl.when(g >= sum_slots)
                def _():
                    go_back(g - sum_slots).wait_send()
                    pl.when(jnp.logical_not(is_end))(lambda: go_out(g - sum_slots).wait_send())

                @pl.when(is_mid)
                def _():
                    go_mid(g).wait_recv()
                    value = (mine[s] + crossed[s].astype(f32)).astype(bf16)
                    rows_w[g // n, pl.ds(0, own), span(g % n, wide)] = value

                pl.when(jnp.logical_not(is_mid))(lambda: go_out(g).wait_recv())
                pl.when(jnp.logical_not(is_end))(lambda: go_out(g).start())
                go_back(g).start()

            def hand_over(g, k):
                s = g % red_slots
                for turn in range(2):
                    pl.when(g >= red_slots)(
                        lambda turn=turn: red_send(g - red_slots, turn, k).wait_send()
                    )
                    at = held(give[turn][k], k + 1)
                    staged[s, at] = part[s, at].astype(bf16)
                    red_send(g, turn, k).start()

            def turn_tile_of(g):
                s = g % red_slots
                ahead(fetch_turn, g, TURN_BUFFERS)
                cut = rows // DEPTHS

                def some(j):
                    at = span(j, cut)
                    return jnp.dot(
                        rows_w[g // n, :, at], turn_tile[g % TURN_BUFFERS, at], preferred_element_type=f32
                    )

                part[s] = some(0)

                def more(j, c):
                    part[s] += some(j)
                    return c

                lax.fori_loop(1, DEPTHS, more, 0)
                hand_over(g, 0)

            def red_in(g, k):
                s = g % red_slots
                cut = span(g % n, thin)
                for turn in range(2):
                    red_send(g, turn, k).wait_recv()
                    at = held(keep[turn][k + 1], k + 1)
                    value = part[s, at] + got[k][s, turn].astype(f32)
                    if k + 1 < bits:
                        part[s, at] = value
                    else:
                        pl.when(g >= red_slots)(
                            lambda turn=turn: all_send(g - red_slots, turn, k).wait_send()
                        )
                        scale = eigen_rows[g // n, at] * in_row[:, cut]
                        scaled[g // n, at, cut] = (value / (scale + damping)).astype(bf16)
                        all_send(g, turn, k).start()
                if k + 1 < bits:
                    hand_over(g, k + 1)

            def red_out(g, k):
                for turn in range(2):
                    all_send(g, turn, k).wait_recv()
                    if k > 0:
                        pl.when(g >= red_slots)(
                            lambda turn=turn: all_send(g - red_slots, turn, k - 1).wait_send()
                        )
                        all_send(g, turn, k - 1).start()

            def out_tile_of(g):
                s = g % scatter_slots
                ahead(fetch_out, g, OUT_BUFFERS)
                pl.when(g >= scatter_slots)(lambda: out_swap(g - scatter_slots).wait_send())
                whole = lax.dot_general(
                    scaled[g // n], out_tile[g % OUT_BUFFERS], (((1,), (1,)), ((), ())),
                    preferred_element_type=f32,
                )
                omine[s] = whole[:own]
                oother[s] = whole[own:].astype(bf16)
                out_swap(g).start()

            def each(start, stop, f):
                lax.fori_loop(start, stop, lambda b, c: (f(b), c)[1], 0)

            def chip_sum(g):
                s = g % scatter_slots
                out_swap(g).wait_recv()
                omine[s] += oswapped[s].astype(f32)

            def flow(g, go, send, get, first, start, stop):
                s = g % scatter_slots

                @pl.when(first)
                def _():
                    def plain(b):
                        pl.when(g >= scatter_slots)(lambda: go(g - scatter_slots, b).wait_send())
                        send[s, span(b, r)] = omine[s, span(b, r)].astype(bf16)
                        go(g, b).start()

                    each(start, stop, plain)

                @pl.when(jnp.logical_not(first))
                def _():
                    go(g, chip).wait_recv()
                    mid = span(chip, r)

                    def through(b):
                        pl.when(g >= scatter_slots)(lambda: go(g - scatter_slots, b).wait_send())
                        go(g, b).wait_recv()
                        at = span(b, r)
                        send[s, at] = (omine[s, at] + get[s, at].astype(f32)).astype(bf16)
                        go(g, b).start()

                    each(start, stop, through)
                    omine[s, mid] += get[s, mid].astype(f32)

            def finish(g):
                s = g % scatter_slots
                out[span(g // n, r), span(g % n, wide)] = omine[s, span(chip, r)].astype(bf16)

            def when(t, starts, lag, f):
                u = t - lag
                for q in range(QUERY_CHUNKS):
                    num, den = TURN_RATE if starts is turn_at and q == 0 else (1, 1)

                    def first(u):
                        return jnp.clip(u - starts[q], 0, n) * num // den

                    lo, hi = jnp.minimum(first(u), n), jnp.minimum(first(u + 1), n)
                    each(lo + q * n, hi + q * n, f)

            def begin(fetch, buffers):
                for g in range(buffers - 1):
                    fetch(g).start()

            begin(fetch_pick, PICK_BUFFERS)
            begin(fetch_grad, BUFFERS)
            out_row[...] = out_eigen[pl.ds(layer[0], 1)]
            in_row[...] = in_eigen[pl.ds(layer[0], 1)]
            each(0, picks, pick)
            begin(fetch_turn, TURN_BUFFERS)
            begin(fetch_out, OUT_BUFFERS)
            edge = (chip == 0) | (chip == chips - 1)
            pl.semaphore_wait(barrier, 1 + bits + jnp.where(edge, 1, 2))
            row_at = [q * n for q in range(QUERY_CHUNKS)]

            share = -(-picks * (QUERY_CHUNKS - 1) // (n - 1))

            def tick(t):
                start = jnp.minimum(picks + t * share, QUERY_CHUNKS * picks)
                each(start, jnp.minimum(start + share, QUERY_CHUNKS * picks), pick)
                when(t, row_at, 0, rows_tile)
                when(t, turn_at, 0, turn_tile_of)
                when(t, out_at, 0, out_tile_of)
                when(t, row_at, 1 + IN_LAG * depth_in, sum_in)
                mid_at = 1 + IN_LAG * (half - 1) + MID_LAG
                when(t, row_at, mid_at + OUT_LAG * (half - 1 - depth_in), sum_out)
                when(t, row_at, sum_lag, lambda g: go_back(g).wait_recv())
                when(t, out_at, 1, chip_sum)
                when(
                    t, out_at, 1 + SCATTER_LAG * chip,
                    lambda g: flow(g, go_right, rsent, rgot, chip == 0, chip + 1, chips),
                )
                when(
                    t, out_at, 1 + SCATTER_LAG * (chips - 1 - chip),
                    lambda g: flow(g, go_left, lsent, lgot, chip == chips - 1, 0, chip),
                )
                for k in range(bits):
                    when(t, turn_at, RED_LAG * (1 + k), lambda g, k=k: red_in(g, k))
                for k in range(bits):
                    when(
                        t, turn_at, RED_LAG * (1 + bits + k),
                        lambda g, k=k: red_out(g, bits - 1 - k),
                    )
                last = 1 + SCATTER_LAG * jnp.maximum(chip, chips - 1 - chip)
                when(t, out_at, last, finish)

            each(0, ticks, tick)

            def drain_sum(g):
                swap(g).wait_send()
                go_back(g).wait_send()
                pl.when(is_mid)(lambda: go_mid(g).wait_send())
                pl.when(jnp.logical_not(is_mid))(lambda: go_in(g).wait_send())
                pl.when(jnp.logical_not(is_end))(lambda: go_out(g).wait_send())

            def drain_red(g):
                for turn in range(2):
                    for k in range(bits):
                        red_send(g, turn, k).wait_send()
                        all_send(g, turn, k).wait_send()

            def drain_scatter(g):
                out_swap(g).wait_send()
                each(chip + 1, chips, lambda b: go_right(g, b).wait_send())
                each(0, chip, lambda b: go_left(g, b).wait_send())

            each(max(0, total - sum_slots), total, drain_sum)
            each(max(0, total - red_slots), total, drain_red)
            each(max(0, total - scatter_slots), total, drain_scatter)

        vmem = pl.BlockSpec(memory_space=pltpu.VMEM)
        hbm = pl.BlockSpec(memory_space=pl.ANY)
        smem = pl.BlockSpec(memory_space=pltpu.SMEM)

        def sems(count):
            return pltpu.SemaphoreType.DMA((count,))

        def slots(count, *shape):
            return pltpu.VMEM((count, *shape), bf16)

        return pl.pallas_call(
            kernel,
            out_shape=jax.ShapeDtypeStruct((QUERY_CHUNKS * r, rows), bf16),
            in_specs=[smem, vmem, hbm, hbm, hbm, vmem, vmem],
            out_specs=vmem,
            scratch_shapes=[
                slots(QUERY_CHUNKS, per, depth),
                pltpu.VMEM((1, units), f32),
                pltpu.VMEM((1, cols), f32),
                pltpu.VMEM((per, 128), f32),
                pltpu.VMEM((QUERY_CHUNKS, per, 1), f32),
                slots(PICK_BUFFERS, depth, wide),
                slots(BUFFERS, depth, wide),
            ]
            + [pltpu.VMEM((sum_slots, own, wide), f32)]
            + [slots(sum_slots, own, wide)] * 5
            + [
                slots(QUERY_CHUNKS, per, rows),
                slots(TURN_BUFFERS, rows, thin),
                pltpu.VMEM((red_slots, per, thin), f32),
                slots(red_slots, per, thin),
            ]
            + [slots(red_slots, 2, stream >> (k + 1), thin) for k in range(bits)]
            + [
                slots(QUERY_CHUNKS, per, cols),
                slots(OUT_BUFFERS, wide, cols),
                pltpu.VMEM((scatter_slots, own, wide), f32),
            ]
            + [slots(scatter_slots, own, wide)] * 6
            + [sems(PICK_BUFFERS), sems(BUFFERS), sems(TURN_BUFFERS), sems(OUT_BUFFERS)]
            + [sems(sum_slots)] * 10
            + [sems(2 * bits * red_slots)] * 4
            + [sems(scatter_slots)] * 2
            + [sems(scatter_slots * chips)] * 4,
            compiler_params=pltpu.CompilerParams(
                collective_id=0, has_side_effects=True, vmem_limit_bytes=62 * 1024 * 1024
            ),
        )

    def per_device(query_ids, layer_index, gradient, out_basis, in_basis, out_eigen, in_eigen):
        core = lax.axis_index("loop") % 2
        queries = query_ids.shape[0]
        depth, rows = gradient.shape
        cols = in_basis.shape[1]
        r = queries // loop // QUERY_CHUNKS
        per = queries // QUERY_CHUNKS
        ids = query_ids.reshape(chips, 2, QUERY_CHUNKS, r).transpose(2, 1, 0, 3)
        ids = jnp.where(core == 0, ids, ids[:, ::-1]).reshape(-1)
        ids = ids.reshape(QUERY_CHUNKS, per, 1)
        units = out_basis.shape[1]
        run = product(per, per // 2, r, depth, units, rows, cols, piece_count(rows, cols))
        return run(layer_index, ids, gradient, out_basis, in_basis, out_eigen, in_eigen)

    return per_device


def solution(mesh):
    return jax.shard_map(
        make(mesh),
        mesh=mesh,
        in_specs=(
            P(),
            P(),
            P("loop", "red"),
            P("loop", None),
            P("red", "loop"),
            P(),
            P(None, "loop"),
        ),
        out_specs=P("loop", "red"),
        check_vma=False,
    )
```

```python
import jax
import jax.numpy as jnp
from jax import lax
from jax.experimental import pallas as pl
from jax.experimental.pallas import tpu as pltpu
from jax.sharding import PartitionSpec as P

damping = 0.05
QUERY_CHUNKS = 2
PIECES = 14
IN_LAG, MID_LAG, OUT_LAG, SCATTER_LAG = 2, 2, 2, 2
BUFFERS = 3
PICK_BUFFERS, TURN_BUFFERS, OUT_BUFFERS = 4, 2, 2
PICK_WIDE = 1024
DEPTHS = 2
RED_LAG = 2


def piece_count(*sizes):
    count = PIECES
    while any(size % count or (size // count) % 128 for size in sizes):
        count -= 1
    return count


def make(mesh):
    loop, red = mesh.shape["loop"], mesh.shape["red"]
    chips = loop // 2
    half = chips // 2
    bits = red.bit_length() - 1
    f32, bf16 = jnp.float32, jnp.bfloat16

    def product(per, own, r, depth, units, rows, cols, n):
        wide, thin = rows // n, cols // n
        total = QUERY_CHUNKS * n
        pick_wide = min(PICK_WIDE, units)
        picks = units // pick_wide
        sum_lag = 2 + (IN_LAG + OUT_LAG) * (half - 1) + MID_LAG
        sum_slots = sum_lag + 1
        red_lag = 2 * bits * RED_LAG
        red_slots = red_lag + 1
        scatter_lag = 1 + (chips - 1) * SCATTER_LAG
        scatter_slots = scatter_lag + 1
        stream = per // 2
        turn_at, out_at = [], []
        for q in range(QUERY_CHUNKS):
            ready = (q + 1) * n + sum_lag
            turn_at.append(max(ready, turn_at[-1] + n) if q else ready)
            ready = turn_at[-1] + n + red_lag
            out_at.append(max(ready, out_at[-1] + n) if q else ready)
        ticks = out_at[-1] + n + scatter_lag

        def kernel(
            layer, ids, gradient, out_basis, in_basis, out_eigen, in_eigen, out,
            selected, out_row, in_row, eigen_sum, eigen_rows, pick_tile, grad_tile, mine, other, swapped, arrived, crossed, sent, rows_w,
            turn_tile, part, staged, *rest,
        ):
            got, rest = rest[:bits], rest[bits:]
            (
                scaled, out_tile, omine, oother, oswapped, rsent, lsent, rgot, lgot,
                pick_sem, grad_sem, turn_sem, tile_sem,
                swap_s, swap_r, in_s, in_r, mid_s, mid_r, out_s, out_r, back_s, back_r,
                red_s, red_r, all_s, all_r,
                oswap_s, oswap_r, right_s, right_r, left_s, left_r,
            ) = rest
            me = lax.axis_index("loop")
            here = lax.axis_index("red")
            chip, core = me // 2, me % 2
            left = chip < half
            depth_in = jnp.where(left, chip, chips - 1 - chip)
            is_mid = depth_in == half - 1
            is_end = depth_in == 0
            partner = chip * 2 + 1 - core
            inner = jnp.where(left, me + 2, me - 2)
            outer = jnp.where(left, me - 2, me + 2)

            def remote(src, dst, s, r, k, to):
                return pltpu.make_async_remote_copy(
                    src_ref=src, dst_ref=dst, send_sem=s.at[k], recv_sem=r.at[k],
                    device_id=to, device_id_type=pl.DeviceIdType.MESH,
                )

            def span(i, size):
                return pl.ds(pl.multiple_of(i * size, size), size)

            def swap(g):
                s = g % sum_slots
                return remote(other.at[s], swapped.at[s], swap_s, swap_r, s, {"loop": partner})

            def go_in(g):
                s = g % sum_slots
                return remote(sent.at[s], arrived.at[s], in_s, in_r, s, {"loop": inner})

            def go_mid(g):
                s = g % sum_slots
                return remote(sent.at[s], crossed.at[s], mid_s, mid_r, s, {"loop": inner})

            def go_out(g):
                at = rows_w.at[g // n, pl.ds(0, own), span(g % n, wide)]
                return remote(at, at, out_s, out_r, g % sum_slots, {"loop": outer})

            def go_back(g):
                cut = span(g % n, wide)
                return remote(
                    rows_w.at[g // n, pl.ds(0, own), cut], rows_w.at[g // n, pl.ds(own, own), cut],
                    back_s, back_r, g % sum_slots, {"loop": partner},
                )

            order = [[(k + turn) % bits for k in range(bits)] for turn in range(2)]
            keep, give = [], []
            for turn in range(2):
                at = turn * stream
                keep.append([at])
                give.append([])
                for k, bit in enumerate(order[turn]):
                    size = stream >> (k + 1)
                    mine_is = (here // (1 << bit)) % 2
                    give[turn].append(at + (1 - mine_is) * size)
                    at = at + mine_is * size
                    keep[turn].append(at)

            def across(turn, k):
                bit = 1 << order[turn][k]
                up = (here // bit) % 2
                return {"red": here + bit - 2 * bit * up}

            def held(start, k):
                size = stream >> k
                return pl.ds(pl.multiple_of(start, size), size)

            def red_send(g, turn, k):
                s = g % red_slots
                return remote(
                    staged.at[s, held(give[turn][k], k + 1)], got[k].at[s, turn],
                    red_s, red_r, (k * 2 + turn) * red_slots + s, across(turn, k),
                )

            def all_send(g, turn, k):
                at = scaled.at[g // n, held(keep[turn][k + 1], k + 1), span(g % n, thin)]
                return remote(
                    at, at, all_s, all_r, (k * 2 + turn) * red_slots + g % red_slots, across(turn, k)
                )

            def out_swap(g):
                s = g % scatter_slots
                return remote(oother.at[s], oswapped.at[s], oswap_s, oswap_r, s, {"loop": partner})

            def go_right(g, b):
                s = g % scatter_slots
                return remote(
                    rsent.at[s, span(b, r)], rgot.at[s, span(b, r)], right_s, right_r,
                    s * chips + b, {"loop": me + 2},
                )

            def go_left(g, b):
                s = g % scatter_slots
                return remote(
                    lsent.at[s, span(b, r)], lgot.at[s, span(b, r)], left_s, left_r,
                    s * chips + b, {"loop": me - 2},
                )

            barrier = pltpu.get_barrier_semaphore()

            def greet(to):
                pl.semaphore_signal(
                    barrier, inc=1, device_id=to, device_id_type=pl.DeviceIdType.MESH
                )

            greet({"loop": partner})
            for k in range(bits):
                greet(across(0, k))
            pl.when(chip > 0)(lambda: greet({"loop": me - 2}))
            pl.when(chip < chips - 1)(lambda: greet({"loop": me + 2}))
            def fetch_grad(g):
                return pltpu.make_async_copy(
                    gradient.at[:, span(g % n, wide)], grad_tile.at[g % BUFFERS], grad_sem.at[g % BUFFERS]
                )

            def fetch_turn(g):
                return pltpu.make_async_copy(
                    in_basis.at[:, span(g % n, thin)], turn_tile.at[g % TURN_BUFFERS], turn_sem.at[g % TURN_BUFFERS]
                )

            def fetch_out(g):
                return pltpu.make_async_copy(
                    in_basis.at[span(g % n, wide)], out_tile.at[g % OUT_BUFFERS], tile_sem.at[g % OUT_BUFFERS]
                )

            def fetch_pick(g):
                return pltpu.make_async_copy(
                    out_basis.at[:, span(g % picks, pick_wide)],
                    pick_tile.at[g % PICK_BUFFERS], pick_sem.at[g % PICK_BUFFERS],
                )

            def ahead(fetch, g, buffers, total=total):
                fetch(g).wait()
                more = g + buffers - 1
                pl.when(more < total)(lambda: fetch(more).start())

            def pick(g):
                q, k = g // picks, g % picks
                ahead(fetch_pick, g, PICK_BUFFERS, QUERY_CHUNKS * picks)
                at = lax.broadcasted_iota(jnp.int32, (per, pick_wide), 1) + k * pick_wide
                hot = ids[q] == at
                values = lax.dot_general(
                    hot.astype(bf16), pick_tile[g % PICK_BUFFERS], (((1,), (1,)), ((), ())),
                    preferred_element_type=f32,
                ).astype(bf16)
                eigen = jnp.where(hot, out_row[:, span(k, pick_wide)], 0.0)
                eigen = sum(eigen[:, c : c + 128] for c in range(0, pick_wide, 128))

                @pl.when(k == 0)
                def _():
                    selected[q] = values
                    eigen_sum[...] = eigen

                @pl.when(k > 0)
                def _():
                    selected[q] += values
                    eigen_sum[...] += eigen

                @pl.when(k == picks - 1)
                def _():
                    eigen_rows[q] = jnp.sum(eigen_sum[...], axis=1, keepdims=True)

            def rows_tile(g):
                s = g % sum_slots
                ahead(fetch_grad, g, BUFFERS)
                whole = jnp.dot(
                    selected[g // n], grad_tile[g % BUFFERS], preferred_element_type=f32
                )
                pl.when(g >= sum_slots)(lambda: swap(g - sum_slots).wait_send())
                mine[s] = whole[:own]
                other[s] = whole[own:].astype(bf16)
                swap(g).start()

            def sum_in(g):
                s = g % sum_slots

                @pl.when(g >= sum_slots)
                def _():
                    pl.when(is_mid)(lambda: go_mid(g - sum_slots).wait_send())
                    pl.when(jnp.logical_not(is_mid))(lambda: go_in(g - sum_slots).wait_send())

                swap(g).wait_recv()

                @pl.when(is_end)
                def _():
                    value = mine[s] + swapped[s].astype(f32)
                    mine[s] = value
                    sent[s] = value.astype(bf16)

                @pl.when(jnp.logical_not(is_end))
                def _():
                    go_in(g).wait_recv()
                    value = mine[s] + swapped[s].astype(f32) + arrived[s].astype(f32)
                    mine[s] = value
                    sent[s] = value.astype(bf16)

                pl.when(is_mid)(lambda: go_mid(g).start())
                pl.when(jnp.logical_not(is_mid))(lambda: go_in(g).start())

            def sum_out(g):
                s = g % sum_slots

                @pl.when(g >= sum_slots)
                def _():
                    go_back(g - sum_slots).wait_send()
                    pl.when(jnp.logical_not(is_end))(lambda: go_out(g - sum_slots).wait_send())

                @pl.when(is_mid)
                def _():
                    go_mid(g).wait_recv()
                    value = (mine[s] + crossed[s].astype(f32)).astype(bf16)
                    rows_w[g // n, pl.ds(0, own), span(g % n, wide)] = value

                pl.when(jnp.logical_not(is_mid))(lambda: go_out(g).wait_recv())
                pl.when(jnp.logical_not(is_end))(lambda: go_out(g).start())
                go_back(g).start()

            def hand_over(g, k):
                s = g % red_slots
                for turn in range(2):
                    pl.when(g >= red_slots)(
                        lambda turn=turn: red_send(g - red_slots, turn, k).wait_send()
                    )
                    at = held(give[turn][k], k + 1)
                    staged[s, at] = part[s, at].astype(bf16)
                    red_send(g, turn, k).start()

            def turn_tile_of(g):
                s = g % red_slots
                ahead(fetch_turn, g, TURN_BUFFERS)
                cut = rows // DEPTHS

                def some(j):
                    at = span(j, cut)
                    return jnp.dot(
                        rows_w[g // n, :, at], turn_tile[g % TURN_BUFFERS, at], preferred_element_type=f32
                    )

                part[s] = some(0)

                def more(j, c):
                    part[s] += some(j)
                    return c

                lax.fori_loop(1, DEPTHS, more, 0)
                hand_over(g, 0)

            def red_in(g, k):
                s = g % red_slots
                cut = span(g % n, thin)
                for turn in range(2):
                    red_send(g, turn, k).wait_recv()
                    at = held(keep[turn][k + 1], k + 1)
                    value = part[s, at] + got[k][s, turn].astype(f32)
                    if k + 1 < bits:
                        part[s, at] = value
                    else:
                        pl.when(g >= red_slots)(
                            lambda turn=turn: all_send(g - red_slots, turn, k).wait_send()
                        )
                        scale = eigen_rows[g // n, at] * in_row[:, cut]
                        scaled[g // n, at, cut] = (value / (scale + damping)).astype(bf16)
                        all_send(g, turn, k).start()
                if k + 1 < bits:
                    hand_over(g, k + 1)

            def red_out(g, k):
                for turn in range(2):
                    all_send(g, turn, k).wait_recv()
                    if k > 0:
                        pl.when(g >= red_slots)(
                            lambda turn=turn: all_send(g - red_slots, turn, k - 1).wait_send()
                        )
                        all_send(g, turn, k - 1).start()

            def out_tile_of(g):
                s = g % scatter_slots
                ahead(fetch_out, g, OUT_BUFFERS)
                pl.when(g >= scatter_slots)(lambda: out_swap(g - scatter_slots).wait_send())
                whole = lax.dot_general(
                    scaled[g // n], out_tile[g % OUT_BUFFERS], (((1,), (1,)), ((), ())),
                    preferred_element_type=f32,
                )
                omine[s] = whole[:own]
                oother[s] = whole[own:].astype(bf16)
                out_swap(g).start()

            def each(start, stop, f):
                lax.fori_loop(start, stop, lambda b, c: (f(b), c)[1], 0)

            def chip_sum(g):
                s = g % scatter_slots
                out_swap(g).wait_recv()
                omine[s] += oswapped[s].astype(f32)

            def flow(g, go, send, get, first, start, stop):
                s = g % scatter_slots

                @pl.when(first)
                def _():
                    def plain(b):
                        pl.when(g >= scatter_slots)(lambda: go(g - scatter_slots, b).wait_send())
                        send[s, span(b, r)] = omine[s, span(b, r)].astype(bf16)
                        go(g, b).start()

                    each(start, stop, plain)

                @pl.when(jnp.logical_not(first))
                def _():
                    go(g, chip).wait_recv()
                    mid = span(chip, r)

                    def through(b):
                        pl.when(g >= scatter_slots)(lambda: go(g - scatter_slots, b).wait_send())
                        go(g, b).wait_recv()
                        at = span(b, r)
                        send[s, at] = (omine[s, at] + get[s, at].astype(f32)).astype(bf16)
                        go(g, b).start()

                    each(start, stop, through)
                    omine[s, mid] += get[s, mid].astype(f32)

            def finish(g):
                s = g % scatter_slots
                out[span(g // n, r), span(g % n, wide)] = omine[s, span(chip, r)].astype(bf16)

            def when(t, starts, lag, f):
                u = t - lag
                i, g = u - starts[0], u - starts[0]
                for q in range(1, QUERY_CHUNKS):
                    i = jnp.where(u >= starts[q], u - starts[q], i)
                    g = jnp.where(u >= starts[q], u - starts[q] + q * n, g)
                pl.when((i >= 0) & (i < n))(lambda: f(g))

            def begin(fetch, buffers):
                for g in range(buffers - 1):
                    fetch(g).start()

            begin(fetch_pick, PICK_BUFFERS)
            begin(fetch_grad, BUFFERS)
            out_row[...] = out_eigen[pl.ds(layer[0], 1)]
            in_row[...] = in_eigen[pl.ds(layer[0], 1)]
            each(0, picks, pick)
            begin(fetch_turn, TURN_BUFFERS)
            begin(fetch_out, OUT_BUFFERS)
            edge = (chip == 0) | (chip == chips - 1)
            pl.semaphore_wait(barrier, 1 + bits + jnp.where(edge, 1, 2))
            row_at = [q * n for q in range(QUERY_CHUNKS)]

            share = -(-picks * (QUERY_CHUNKS - 1) // (n - 1))

            def tick(t):
                start = jnp.minimum(picks + t * share, QUERY_CHUNKS * picks)
                each(start, jnp.minimum(start + share, QUERY_CHUNKS * picks), pick)
                when(t, row_at, 0, rows_tile)
                when(t, turn_at, 0, turn_tile_of)
                when(t, out_at, 0, out_tile_of)
                when(t, row_at, 1 + IN_LAG * depth_in, sum_in)
                mid_at = 1 + IN_LAG * (half - 1) + MID_LAG
                when(t, row_at, mid_at + OUT_LAG * (half - 1 - depth_in), sum_out)
                when(t, row_at, sum_lag, lambda g: go_back(g).wait_recv())
                when(t, out_at, 1, chip_sum)
                when(
                    t, out_at, 1 + SCATTER_LAG * chip,
                    lambda g: flow(g, go_right, rsent, rgot, chip == 0, chip + 1, chips),
                )
                when(
                    t, out_at, 1 + SCATTER_LAG * (chips - 1 - chip),
                    lambda g: flow(g, go_left, lsent, lgot, chip == chips - 1, 0, chip),
                )
                for k in range(bits):
                    when(t, turn_at, RED_LAG * (1 + k), lambda g, k=k: red_in(g, k))
                for k in range(bits):
                    when(
                        t, turn_at, RED_LAG * (1 + bits + k),
                        lambda g, k=k: red_out(g, bits - 1 - k),
                    )
                last = 1 + SCATTER_LAG * jnp.maximum(chip, chips - 1 - chip)
                when(t, out_at, last, finish)

            each(0, ticks, tick)

            def drain_sum(g):
                swap(g).wait_send()
                go_back(g).wait_send()
                pl.when(is_mid)(lambda: go_mid(g).wait_send())
                pl.when(jnp.logical_not(is_mid))(lambda: go_in(g).wait_send())
                pl.when(jnp.logical_not(is_end))(lambda: go_out(g).wait_send())

            def drain_red(g):
                for turn in range(2):
                    for k in range(bits):
                        red_send(g, turn, k).wait_send()
                        all_send(g, turn, k).wait_send()

            def drain_scatter(g):
                out_swap(g).wait_send()
                each(chip + 1, chips, lambda b: go_right(g, b).wait_send())
                each(0, chip, lambda b: go_left(g, b).wait_send())

            each(max(0, total - sum_slots), total, drain_sum)
            each(max(0, total - red_slots), total, drain_red)
            each(max(0, total - scatter_slots), total, drain_scatter)

        vmem = pl.BlockSpec(memory_space=pltpu.VMEM)
        hbm = pl.BlockSpec(memory_space=pl.ANY)
        smem = pl.BlockSpec(memory_space=pltpu.SMEM)

        def sems(count):
            return pltpu.SemaphoreType.DMA((count,))

        def slots(count, *shape):
            return pltpu.VMEM((count, *shape), bf16)

        return pl.pallas_call(
            kernel,
            out_shape=jax.ShapeDtypeStruct((QUERY_CHUNKS * r, rows), bf16),
            in_specs=[smem, vmem, hbm, hbm, hbm, vmem, vmem],
            out_specs=vmem,
            scratch_shapes=[
                slots(QUERY_CHUNKS, per, depth),
                pltpu.VMEM((1, units), f32),
                pltpu.VMEM((1, cols), f32),
                pltpu.VMEM((per, 128), f32),
                pltpu.VMEM((QUERY_CHUNKS, per, 1), f32),
                slots(PICK_BUFFERS, depth, pick_wide),
                slots(BUFFERS, depth, wide),
            ]
            + [pltpu.VMEM((sum_slots, own, wide), f32)]
            + [slots(sum_slots, own, wide)] * 5
            + [
                slots(QUERY_CHUNKS, per, rows),
                slots(TURN_BUFFERS, rows, thin),
                pltpu.VMEM((red_slots, per, thin), f32),
                slots(red_slots, per, thin),
            ]
            + [slots(red_slots, 2, stream >> (k + 1), thin) for k in range(bits)]
            + [
                slots(QUERY_CHUNKS, per, cols),
                slots(OUT_BUFFERS, wide, cols),
                pltpu.VMEM((scatter_slots, own, wide), f32),
            ]
            + [slots(scatter_slots, own, wide)] * 6
            + [sems(PICK_BUFFERS), sems(BUFFERS), sems(TURN_BUFFERS), sems(OUT_BUFFERS)]
            + [sems(sum_slots)] * 10
            + [sems(2 * bits * red_slots)] * 4
            + [sems(scatter_slots)] * 2
            + [sems(scatter_slots * chips)] * 4,
            compiler_params=pltpu.CompilerParams(
                collective_id=0, has_side_effects=True, vmem_limit_bytes=62 * 1024 * 1024
            ),
        )

    def per_device(query_ids, layer_index, gradient, out_basis, in_basis, out_eigen, in_eigen):
        core = lax.axis_index("loop") % 2
        queries = query_ids.shape[0]
        depth, rows = gradient.shape
        cols = in_basis.shape[1]
        r = queries // loop // QUERY_CHUNKS
        per = queries // QUERY_CHUNKS
        ids = query_ids.reshape(chips, 2, QUERY_CHUNKS, r).transpose(2, 1, 0, 3)
        ids = jnp.where(core == 0, ids, ids[:, ::-1]).reshape(-1)
        ids = ids.reshape(QUERY_CHUNKS, per, 1)
        units = out_basis.shape[1]
        run = product(per, per // 2, r, depth, units, rows, cols, piece_count(rows, cols))
        return run(layer_index, ids, gradient, out_basis, in_basis, out_eigen, in_eigen)

    return per_device


def solution(mesh):
    return jax.shard_map(
        make(mesh),
        mesh=mesh,
        in_specs=(
            P(),
            P(),
            P("loop", "red"),
            P("loop", None),
            P("red", "loop"),
            P(),
            P(None, "loop"),
        ),
        out_specs=P("loop", "red"),
        check_vma=False,
    )
```

```python
import jax
import jax.numpy as jnp
from jax import lax
from jax.experimental import pallas as pl
from jax.experimental.pallas import tpu as pltpu
from jax.sharding import PartitionSpec as P

damping = 0.05
QUERY_CHUNKS = 2
PIECES = 14
IN_LAG, MID_LAG, OUT_LAG, SCATTER_LAG = 2, 2, 2, 2
BUFFERS = 3
PICK_BUFFERS, TURN_BUFFERS, OUT_BUFFERS = 2, 2, 2
PICK_WIDE = 2048
DEPTHS = 2
RED_LAG = 2


def piece_count(*sizes):
    count = PIECES
    while any(size % count or (size // count) % 128 for size in sizes):
        count -= 1
    return count


def make(mesh):
    loop, red = mesh.shape["loop"], mesh.shape["red"]
    chips = loop // 2
    half = chips // 2
    bits = red.bit_length() - 1
    f32, bf16 = jnp.float32, jnp.bfloat16

    def product(per, own, r, depth, units, rows, cols, n):
        wide, thin = rows // n, cols // n
        total = QUERY_CHUNKS * n
        pick_wide = min(PICK_WIDE, units)
        picks = units // pick_wide
        sum_lag = 2 + (IN_LAG + OUT_LAG) * (half - 1) + MID_LAG
        sum_slots = sum_lag + 1
        red_lag = 2 * bits * RED_LAG
        red_slots = red_lag + 1
        scatter_lag = 1 + (chips - 1) * SCATTER_LAG
        scatter_slots = scatter_lag + 1
        stream = per // 2
        turn_at, out_at = [], []
        for q in range(QUERY_CHUNKS):
            ready = (q + 1) * n + sum_lag
            turn_at.append(max(ready, turn_at[-1] + n) if q else ready)
            ready = turn_at[-1] + n + red_lag
            out_at.append(max(ready, out_at[-1] + n) if q else ready)
        ticks = out_at[-1] + n + scatter_lag

        def kernel(
            layer, ids, gradient, out_basis, in_basis, out_eigen, in_eigen, out,
            selected, out_row, in_row, eigen_sum, eigen_rows, pick_tile, grad_tile, mine, other, swapped, arrived, crossed, sent, rows_w,
            turn_tile, part, staged, *rest,
        ):
            got, rest = rest[:bits], rest[bits:]
            (
                scaled, out_tile, omine, oother, oswapped, rsent, lsent, rgot, lgot,
                pick_sem, grad_sem, turn_sem, tile_sem,
                swap_s, swap_r, in_s, in_r, mid_s, mid_r, out_s, out_r, back_s, back_r,
                red_s, red_r, all_s, all_r,
                oswap_s, oswap_r, right_s, right_r, left_s, left_r,
            ) = rest
            me = lax.axis_index("loop")
            here = lax.axis_index("red")
            chip, core = me // 2, me % 2
            left = chip < half
            depth_in = jnp.where(left, chip, chips - 1 - chip)
            is_mid = depth_in == half - 1
            is_end = depth_in == 0
            partner = chip * 2 + 1 - core
            inner = jnp.where(left, me + 2, me - 2)
            outer = jnp.where(left, me - 2, me + 2)

            def remote(src, dst, s, r, k, to):
                return pltpu.make_async_remote_copy(
                    src_ref=src, dst_ref=dst, send_sem=s.at[k], recv_sem=r.at[k],
                    device_id=to, device_id_type=pl.DeviceIdType.MESH,
                )

            def span(i, size):
                return pl.ds(pl.multiple_of(i * size, size), size)

            def swap(g):
                s = g % sum_slots
                return remote(other.at[s], swapped.at[s], swap_s, swap_r, s, {"loop": partner})

            def go_in(g):
                s = g % sum_slots
                return remote(sent.at[s], arrived.at[s], in_s, in_r, s, {"loop": inner})

            def go_mid(g):
                s = g % sum_slots
                return remote(sent.at[s], crossed.at[s], mid_s, mid_r, s, {"loop": inner})

            def go_out(g):
                at = rows_w.at[g // n, pl.ds(0, own), span(g % n, wide)]
                return remote(at, at, out_s, out_r, g % sum_slots, {"loop": outer})

            def go_back(g):
                cut = span(g % n, wide)
                return remote(
                    rows_w.at[g // n, pl.ds(0, own), cut], rows_w.at[g // n, pl.ds(own, own), cut],
                    back_s, back_r, g % sum_slots, {"loop": partner},
                )

            order = [[(k + turn) % bits for k in range(bits)] for turn in range(2)]
            keep, give = [], []
            for turn in range(2):
                at = turn * stream
                keep.append([at])
                give.append([])
                for k, bit in enumerate(order[turn]):
                    size = stream >> (k + 1)
                    mine_is = (here // (1 << bit)) % 2
                    give[turn].append(at + (1 - mine_is) * size)
                    at = at + mine_is * size
                    keep[turn].append(at)

            def across(turn, k):
                bit = 1 << order[turn][k]
                up = (here // bit) % 2
                return {"red": here + bit - 2 * bit * up}

            def held(start, k):
                size = stream >> k
                return pl.ds(pl.multiple_of(start, size), size)

            def red_send(g, turn, k):
                s = g % red_slots
                return remote(
                    staged.at[s, held(give[turn][k], k + 1)], got[k].at[s, turn],
                    red_s, red_r, (k * 2 + turn) * red_slots + s, across(turn, k),
                )

            def all_send(g, turn, k):
                at = scaled.at[g // n, held(keep[turn][k + 1], k + 1), span(g % n, thin)]
                return remote(
                    at, at, all_s, all_r, (k * 2 + turn) * red_slots + g % red_slots, across(turn, k)
                )

            def out_swap(g):
                s = g % scatter_slots
                return remote(oother.at[s], oswapped.at[s], oswap_s, oswap_r, s, {"loop": partner})

            def go_right(g, b):
                s = g % scatter_slots
                return remote(
                    rsent.at[s, span(b, r)], rgot.at[s, span(b, r)], right_s, right_r,
                    s * chips + b, {"loop": me + 2},
                )

            def go_left(g, b):
                s = g % scatter_slots
                return remote(
                    lsent.at[s, span(b, r)], lgot.at[s, span(b, r)], left_s, left_r,
                    s * chips + b, {"loop": me - 2},
                )

            barrier = pltpu.get_barrier_semaphore()

            def greet(to):
                pl.semaphore_signal(
                    barrier, inc=1, device_id=to, device_id_type=pl.DeviceIdType.MESH
                )

            greet({"loop": partner})
            for k in range(bits):
                greet(across(0, k))
            pl.when(chip > 0)(lambda: greet({"loop": me - 2}))
            pl.when(chip < chips - 1)(lambda: greet({"loop": me + 2}))
            def fetch_grad(g):
                return pltpu.make_async_copy(
                    gradient.at[:, span(g % n, wide)], grad_tile.at[g % BUFFERS], grad_sem.at[g % BUFFERS]
                )

            def fetch_turn(g):
                return pltpu.make_async_copy(
                    in_basis.at[:, span(g % n, thin)], turn_tile.at[g % TURN_BUFFERS], turn_sem.at[g % TURN_BUFFERS]
                )

            def fetch_out(g):
                return pltpu.make_async_copy(
                    in_basis.at[span(g % n, wide)], out_tile.at[g % OUT_BUFFERS], tile_sem.at[g % OUT_BUFFERS]
                )

            def fetch_pick(g):
                return pltpu.make_async_copy(
                    out_basis.at[:, span(g % picks, pick_wide)],
                    pick_tile.at[g % PICK_BUFFERS], pick_sem.at[g % PICK_BUFFERS],
                )

            def ahead(fetch, g, buffers, total=total):
                fetch(g).wait()
                more = g + buffers - 1
                pl.when(more < total)(lambda: fetch(more).start())

            def pick(g):
                q, k = g // picks, g % picks
                ahead(fetch_pick, g, PICK_BUFFERS, QUERY_CHUNKS * picks)
                at = lax.broadcasted_iota(jnp.int32, (per, pick_wide), 1) + k * pick_wide
                hot = ids[q] == at
                values = lax.dot_general(
                    hot.astype(bf16), pick_tile[g % PICK_BUFFERS], (((1,), (1,)), ((), ())),
                    preferred_element_type=f32,
                ).astype(bf16)
                eigen = jnp.where(hot, out_row[:, span(k, pick_wide)], 0.0)
                eigen = sum(eigen[:, c : c + 128] for c in range(0, pick_wide, 128))

                @pl.when(k == 0)
                def _():
                    selected[q] = values
                    eigen_sum[...] = eigen

                @pl.when(k > 0)
                def _():
                    selected[q] += values
                    eigen_sum[...] += eigen

                @pl.when(k == picks - 1)
                def _():
                    eigen_rows[q] = jnp.sum(eigen_sum[...], axis=1, keepdims=True)

            def rows_tile(g):
                s = g % sum_slots
                ahead(fetch_grad, g, BUFFERS)
                whole = jnp.dot(
                    selected[g // n], grad_tile[g % BUFFERS], preferred_element_type=f32
                )
                pl.when(g >= sum_slots)(lambda: swap(g - sum_slots).wait_send())
                mine[s] = whole[:own]
                other[s] = whole[own:].astype(bf16)
                swap(g).start()

            def sum_in(g):
                s = g % sum_slots

                @pl.when(g >= sum_slots)
                def _():
                    pl.when(is_mid)(lambda: go_mid(g - sum_slots).wait_send())
                    pl.when(jnp.logical_not(is_mid))(lambda: go_in(g - sum_slots).wait_send())

                swap(g).wait_recv()

                @pl.when(is_end)
                def _():
                    value = mine[s] + swapped[s].astype(f32)
                    mine[s] = value
                    sent[s] = value.astype(bf16)

                @pl.when(jnp.logical_not(is_end))
                def _():
                    go_in(g).wait_recv()
                    value = mine[s] + swapped[s].astype(f32) + arrived[s].astype(f32)
                    mine[s] = value
                    sent[s] = value.astype(bf16)

                pl.when(is_mid)(lambda: go_mid(g).start())
                pl.when(jnp.logical_not(is_mid))(lambda: go_in(g).start())

            def sum_out(g):
                s = g % sum_slots

                @pl.when(g >= sum_slots)
                def _():
                    go_back(g - sum_slots).wait_send()
                    pl.when(jnp.logical_not(is_end))(lambda: go_out(g - sum_slots).wait_send())

                @pl.when(is_mid)
                def _():
                    go_mid(g).wait_recv()
                    value = (mine[s] + crossed[s].astype(f32)).astype(bf16)
                    rows_w[g // n, pl.ds(0, own), span(g % n, wide)] = value

                pl.when(jnp.logical_not(is_mid))(lambda: go_out(g).wait_recv())
                pl.when(jnp.logical_not(is_end))(lambda: go_out(g).start())
                go_back(g).start()

            def hand_over(g, k):
                s = g % red_slots
                for turn in range(2):
                    pl.when(g >= red_slots)(
                        lambda turn=turn: red_send(g - red_slots, turn, k).wait_send()
                    )
                    at = held(give[turn][k], k + 1)
                    staged[s, at] = part[s, at].astype(bf16)
                    red_send(g, turn, k).start()

            def turn_tile_of(g):
                s = g % red_slots
                ahead(fetch_turn, g, TURN_BUFFERS)
                cut = rows // DEPTHS

                def some(j):
                    at = span(j, cut)
                    return jnp.dot(
                        rows_w[g // n, :, at], turn_tile[g % TURN_BUFFERS, at], preferred_element_type=f32
                    )

                part[s] = some(0)

                def more(j, c):
                    part[s] += some(j)
                    return c

                lax.fori_loop(1, DEPTHS, more, 0)
                hand_over(g, 0)

            def red_in(g, k):
                s = g % red_slots
                cut = span(g % n, thin)
                for turn in range(2):
                    red_send(g, turn, k).wait_recv()
                    at = held(keep[turn][k + 1], k + 1)
                    value = part[s, at] + got[k][s, turn].astype(f32)
                    if k + 1 < bits:
                        part[s, at] = value
                    else:
                        pl.when(g >= red_slots)(
                            lambda turn=turn: all_send(g - red_slots, turn, k).wait_send()
                        )
                        scale = eigen_rows[g // n, at] * in_row[:, cut]
                        scaled[g // n, at, cut] = (value / (scale + damping)).astype(bf16)
                        all_send(g, turn, k).start()
                if k + 1 < bits:
                    hand_over(g, k + 1)

            def red_out(g, k):
                for turn in range(2):
                    all_send(g, turn, k).wait_recv()
                    if k > 0:
                        pl.when(g >= red_slots)(
                            lambda turn=turn: all_send(g - red_slots, turn, k - 1).wait_send()
                        )
                        all_send(g, turn, k - 1).start()

            def out_tile_of(g):
                s = g % scatter_slots
                ahead(fetch_out, g, OUT_BUFFERS)
                pl.when(g >= scatter_slots)(lambda: out_swap(g - scatter_slots).wait_send())
                whole = lax.dot_general(
                    scaled[g // n], out_tile[g % OUT_BUFFERS], (((1,), (1,)), ((), ())),
                    preferred_element_type=f32,
                )
                omine[s] = whole[:own]
                oother[s] = whole[own:].astype(bf16)
                out_swap(g).start()

            def each(start, stop, f):
                lax.fori_loop(start, stop, lambda b, c: (f(b), c)[1], 0)

            def chip_sum(g):
                s = g % scatter_slots
                out_swap(g).wait_recv()
                omine[s] += oswapped[s].astype(f32)

            def flow(g, go, send, get, first, start, stop):
                s = g % scatter_slots

                @pl.when(first)
                def _():
                    def plain(b):
                        pl.when(g >= scatter_slots)(lambda: go(g - scatter_slots, b).wait_send())
                        send[s, span(b, r)] = omine[s, span(b, r)].astype(bf16)
                        go(g, b).start()

                    each(start, stop, plain)

                @pl.when(jnp.logical_not(first))
                def _():
                    go(g, chip).wait_recv()
                    mid = span(chip, r)

                    def through(b):
                        pl.when(g >= scatter_slots)(lambda: go(g - scatter_slots, b).wait_send())
                        go(g, b).wait_recv()
                        at = span(b, r)
                        send[s, at] = (omine[s, at] + get[s, at].astype(f32)).astype(bf16)
                        go(g, b).start()

                    each(start, stop, through)
                    omine[s, mid] += get[s, mid].astype(f32)

            def finish(g):
                s = g % scatter_slots
                out[span(g // n, r), span(g % n, wide)] = omine[s, span(chip, r)].astype(bf16)

            def when(t, starts, lag, f):
                u = t - lag
                i, g = u - starts[0], u - starts[0]
                for q in range(1, QUERY_CHUNKS):
                    i = jnp.where(u >= starts[q], u - starts[q], i)
                    g = jnp.where(u >= starts[q], u - starts[q] + q * n, g)
                pl.when((i >= 0) & (i < n))(lambda: f(g))

            def begin(fetch, buffers):
                for g in range(buffers - 1):
                    fetch(g).start()

            begin(fetch_pick, PICK_BUFFERS)
            begin(fetch_grad, BUFFERS)
            out_row[...] = out_eigen[pl.ds(layer[0], 1)]
            in_row[...] = in_eigen[pl.ds(layer[0], 1)]
            each(0, picks, pick)
            begin(fetch_turn, TURN_BUFFERS)
            begin(fetch_out, OUT_BUFFERS)
            edge = (chip == 0) | (chip == chips - 1)
            pl.semaphore_wait(barrier, 1 + bits + jnp.where(edge, 1, 2))
            row_at = [q * n for q in range(QUERY_CHUNKS)]

            share = -(-picks * (QUERY_CHUNKS - 1) // (n - 1))

            def tick(t):
                start = jnp.minimum(picks + t * share, QUERY_CHUNKS * picks)
                each(start, jnp.minimum(start + share, QUERY_CHUNKS * picks), pick)
                when(t, row_at, 0, rows_tile)
                when(t, turn_at, 0, turn_tile_of)
                when(t, out_at, 0, out_tile_of)
                when(t, row_at, 1 + IN_LAG * depth_in, sum_in)
                mid_at = 1 + IN_LAG * (half - 1) + MID_LAG
                when(t, row_at, mid_at + OUT_LAG * (half - 1 - depth_in), sum_out)
                when(t, row_at, sum_lag, lambda g: go_back(g).wait_recv())
                when(t, out_at, 1, chip_sum)
                when(
                    t, out_at, 1 + SCATTER_LAG * chip,
                    lambda g: flow(g, go_right, rsent, rgot, chip == 0, chip + 1, chips),
                )
                when(
                    t, out_at, 1 + SCATTER_LAG * (chips - 1 - chip),
                    lambda g: flow(g, go_left, lsent, lgot, chip == chips - 1, 0, chip),
                )
                for k in range(bits):
                    when(t, turn_at, RED_LAG * (1 + k), lambda g, k=k: red_in(g, k))
                for k in range(bits):
                    when(
                        t, turn_at, RED_LAG * (1 + bits + k),
                        lambda g, k=k: red_out(g, bits - 1 - k),
                    )
                last = 1 + SCATTER_LAG * jnp.maximum(chip, chips - 1 - chip)
                when(t, out_at, last, finish)

            each(0, ticks, tick)

            def drain_sum(g):
                swap(g).wait_send()
                go_back(g).wait_send()
                pl.when(is_mid)(lambda: go_mid(g).wait_send())
                pl.when(jnp.logical_not(is_mid))(lambda: go_in(g).wait_send())
                pl.when(jnp.logical_not(is_end))(lambda: go_out(g).wait_send())

            def drain_red(g):
                for turn in range(2):
                    for k in range(bits):
                        red_send(g, turn, k).wait_send()
                        all_send(g, turn, k).wait_send()

            def drain_scatter(g):
                out_swap(g).wait_send()
                each(chip + 1, chips, lambda b: go_right(g, b).wait_send())
                each(0, chip, lambda b: go_left(g, b).wait_send())

            each(max(0, total - sum_slots), total, drain_sum)
            each(max(0, total - red_slots), total, drain_red)
            each(max(0, total - scatter_slots), total, drain_scatter)

        vmem = pl.BlockSpec(memory_space=pltpu.VMEM)
        hbm = pl.BlockSpec(memory_space=pl.ANY)
        smem = pl.BlockSpec(memory_space=pltpu.SMEM)

        def sems(count):
            return pltpu.SemaphoreType.DMA((count,))

        def slots(count, *shape):
            return pltpu.VMEM((count, *shape), bf16)

        return pl.pallas_call(
            kernel,
            out_shape=jax.ShapeDtypeStruct((QUERY_CHUNKS * r, rows), bf16),
            in_specs=[smem, vmem, hbm, hbm, hbm, vmem, vmem],
            out_specs=vmem,
            scratch_shapes=[
                slots(QUERY_CHUNKS, per, depth),
                pltpu.VMEM((1, units), f32),
                pltpu.VMEM((1, cols), f32),
                pltpu.VMEM((per, 128), f32),
                pltpu.VMEM((QUERY_CHUNKS, per, 1), f32),
                slots(PICK_BUFFERS, depth, pick_wide),
                slots(BUFFERS, depth, wide),
            ]
            + [pltpu.VMEM((sum_slots, own, wide), f32)]
            + [slots(sum_slots, own, wide)] * 5
            + [
                slots(QUERY_CHUNKS, per, rows),
                slots(TURN_BUFFERS, rows, thin),
                pltpu.VMEM((red_slots, per, thin), f32),
                slots(red_slots, per, thin),
            ]
            + [slots(red_slots, 2, stream >> (k + 1), thin) for k in range(bits)]
            + [
                slots(QUERY_CHUNKS, per, cols),
                slots(OUT_BUFFERS, wide, cols),
                pltpu.VMEM((scatter_slots, own, wide), f32),
            ]
            + [slots(scatter_slots, own, wide)] * 6
            + [sems(PICK_BUFFERS), sems(BUFFERS), sems(TURN_BUFFERS), sems(OUT_BUFFERS)]
            + [sems(sum_slots)] * 10
            + [sems(2 * bits * red_slots)] * 4
            + [sems(scatter_slots)] * 2
            + [sems(scatter_slots * chips)] * 4,
            compiler_params=pltpu.CompilerParams(
                collective_id=0, has_side_effects=True, vmem_limit_bytes=62 * 1024 * 1024
            ),
        )

    def per_device(query_ids, layer_index, gradient, out_basis, in_basis, out_eigen, in_eigen):
        core = lax.axis_index("loop") % 2
        queries = query_ids.shape[0]
        depth, rows = gradient.shape
        cols = in_basis.shape[1]
        r = queries // loop // QUERY_CHUNKS
        per = queries // QUERY_CHUNKS
        ids = query_ids.reshape(chips, 2, QUERY_CHUNKS, r).transpose(2, 1, 0, 3)
        ids = jnp.where(core == 0, ids, ids[:, ::-1]).reshape(-1)
        ids = ids.reshape(QUERY_CHUNKS, per, 1)
        units = out_basis.shape[1]
        run = product(per, per // 2, r, depth, units, rows, cols, piece_count(rows, cols))
        return run(layer_index, ids, gradient, out_basis, in_basis, out_eigen, in_eigen)

    return per_device


def solution(mesh):
    return jax.shard_map(
        make(mesh),
        mesh=mesh,
        in_specs=(
            P(),
            P(),
            P("loop", "red"),
            P("loop", None),
            P("red", "loop"),
            P(),
            P(None, "loop"),
        ),
        out_specs=P("loop", "red"),
        check_vma=False,
    )
```
